128 devices in a mesh: px: 8 (over x, core), py: 16 (over z, y).
Axes of the slice: x: 4, y: 4, z: 4, core: 2. Of those that a mesh axis runs over, the one named last changes fastest.
Arguments:
- theta_field: float32 [32, 128, 2048], P(None, 'px', 'py'), may hold values from -6 to 6
- wind_u: float32 [32, 128, 2048], P(None, 'px', 'py'), may hold values from -6 to 6
- wind_v: float32 [32, 128, 2048], P(None, 'px', 'py'), may hold values from -6 to 6
- hyper_coef: float32 [32], replicated, may hold values from 0.002 to 0.02
- damp_coef: float32 [32], replicated, may hold values from 0.05 to 0.4
- obs_cells: int32 [128, 128, 128], P(('px', 'py')), may hold values from 0 to 1918, as said below
- obs_levels: int32 [128, 128, 128], P(('px', 'py')), may hold values from 0 to 30
- obs_bary: float32 [128, 128, 3, 128], P(('px', 'py')), may hold values from 0 to 1, as said below
- obs_vfrac: float32 [128, 128, 128], P(('px', 'py')), may hold values from 0 to 1
- obs_values: float32 [128, 128, 128], P(('px', 'py')), may hold values from -6 to 6
- obs_mask: int32 [128, 128, 128], P(('px', 'py')), may hold values from 0 to 1, as said below
Outputs:
- theta_next: float32 [32, 128, 2048], P(None, 'px', 'py')
- wind_u_next: float32 [32, 128, 2048], P(None, 'px', 'py')
- wind_v_next: float32 [32, 128, 2048], P(None, 'px', 'py')
- departures: float32 [128, 128, 128], P(('px', 'py'))
The draws below stay inside these ranges and needn't reach their ends.
Inputs may be any that keep to these rules, and one draw needn't show every extreme that they name: obs_cells is r * 128 + c with r below 15 and c below 127. `obs_bary`: each row of three weights is positive and sums to one. `obs_mask`: in every draw some destination patch has all 128 slots used from every owner.
All inputs are finite; a program needn't handle non-finite values.
Results may differ from the reference program's by a relative error of at most 0.000084.
Values sent between devices are 32-bit elements; how exact they have to be, the bound alone decides.
No kernel may reach another device: no remote copies, remote signals or barrier semaphores. Data moves between devices by JAX's collectives and lax.ppermute only.
A program may use at most 64 MiB of HBM per device.

```python
import math
import jax
import jax.numpy as jnp

LEV = 32
CX = 16
CY = 128
PATCHES = 128
SLOT = 128
NX = 128
NY = 2048
N_PY = 16


def draw_obs_cells(key, part):
    key_row, key_col = jax.random.split(jax.random.fold_in(key, 11))
    shape = (PATCHES, PATCHES, SLOT)
    rows = jax.random.randint(key_row, shape, 0, CX - 1)
    cols = jax.random.randint(key_col, shape, 0, CY - 1)
    return (rows * CY + cols).astype(jnp.int32)


def draw_obs_bary(key, part):
    raw = jax.random.uniform(jax.random.fold_in(key, 12), (PATCHES, PATCHES, 3, SLOT), jnp.float32, 0.05, 1.0)
    return raw / jnp.sum(raw, axis=2, keepdims=True)


def draw_obs_mask(key, part):
    key_level, key_full, key_slot = jax.random.split(jax.random.fold_in(key, 13), 3)
    levels = jax.random.randint(key_level, (PATCHES,), 250, 1001)
    full_one = jax.random.randint(key_full, (), 0, PATCHES)
    levels = jnp.where(jnp.arange(PATCHES) == full_one, 1000, levels)
    slots = jax.random.randint(key_slot, (PATCHES, PATCHES, SLOT), 0, 1000)
    return (slots < levels[None, :, None]).astype(jnp.int32)


def with_ends(values, key, smallest, top_value):
    index_at = [jax.random.randint(jax.random.fold_in(key, axis), (), 0, length) for axis, length in enumerate(values.shape)]
    longest = values.shape.index(max(values.shape))
    next_to = index_at[:longest] + [(index_at[longest] + 1) % values.shape[longest]] + index_at[longest + 1:]
    return values.at[tuple(index_at)].set(smallest).at[tuple(next_to)].set(top_value)


def level_of(stream_key, shape, cuts, smallest, high):
    gain, own = 1.0, jax.random.fold_in(stream_key, 6)
    for axis_at, blocks in cuts:
        steps = jnp.exp(jax.random.uniform(jax.random.fold_in(own, axis_at), (blocks,), jnp.float32, smallest / len(cuts), high / len(cuts)))
        gain = gain * jnp.repeat(steps, shape[axis_at] // blocks).reshape([-1 if axis == axis_at else 1 for axis in range(len(shape))])
    return gain


def gaussian(stream_key, dims, scale, most, pieces=(), held_as=jnp.bfloat16):
    values = scale * jax.random.normal(stream_key, dims, jnp.float32)
    if pieces:
        values = values * level_of(stream_key, dims, pieces, -0.22, 0.18)
    return jnp.clip(values, -most, most).astype(held_as)


def setup_inputs(seed: int = 0) -> dict:
    keys = jax.random.split(jax.random.key(seed), 12)
    theta_field = gaussian(keys[0], (LEV, NX, NY), 1.0, 6.0, ((1, 8), (2, 16)), jnp.float32)
    wind_u = gaussian(keys[1], (LEV, NX, NY), 1.0, 6.0, ((1, 8), (2, 16)), jnp.float32)
    wind_v = gaussian(keys[2], (LEV, NX, NY), 1.0, 6.0, ((1, 8), (2, 16)), jnp.float32)
    hyper_coef = jnp.clip(jnp.exp(jax.random.uniform(keys[3], (LEV,), jnp.float32, math.log(0.002), math.log(0.02))), 0.002, 0.02)
    damp_coef = jnp.clip(jnp.exp(jax.random.uniform(keys[4], (LEV,), jnp.float32, math.log(0.05), math.log(0.4))), 0.05, 0.4)
    obs_cells = draw_obs_cells(jax.random.fold_in(keys[11], 71), 0)
    obs_levels = with_ends(jax.random.randint(keys[6], (PATCHES, PATCHES, SLOT), 0, LEV - 1), jax.random.fold_in(keys[6], 1), 0, (LEV - 1) - 1).astype(jnp.int32)
    obs_bary = draw_obs_bary(jax.random.fold_in(keys[11], 71), 0)
    obs_vfrac = jnp.clip(1.0 * jax.random.uniform(keys[8], (PATCHES, PATCHES, SLOT), jnp.float32) ** level_of(keys[8], (PATCHES, PATCHES, SLOT), ((0, 128),), -0.2, 0.2), 0.0, 1.0)
    obs_values = gaussian(keys[9], (PATCHES, PATCHES, SLOT), 1.0, 6.0, ((0, 128),), jnp.float32)
    obs_mask = draw_obs_mask(jax.random.fold_in(keys[11], 71), 0)
    return dict(theta_field=theta_field, wind_u=wind_u, wind_v=wind_v, hyper_coef=hyper_coef, damp_coef=damp_coef, obs_cells=obs_cells, obs_levels=obs_levels, obs_bary=obs_bary, obs_vfrac=obs_vfrac, obs_values=obs_values, obs_mask=obs_mask)


def roll_view(field, step_i, step_j):
    return jnp.roll(field, (-step_i, -step_j), axis=(-2, -1))


def laplace(field):
    total = roll_view(field, 1, 0) + roll_view(field, -1, 0)
    total = total + roll_view(field, 0, 1) + roll_view(field, 0, -1)
    total = total + roll_view(field, 1, -1) + roll_view(field, -1, 1)
    return total - 6.0 * field


def diff_x(field):
    return (roll_view(field, 1, 0) - roll_view(field, -1, 0)) * 0.5


def diff_y(field):
    return (roll_view(field, 0, 1) - roll_view(field, 0, -1)) * 0.5


def reference(theta_field, wind_u, wind_v, hyper_coef, damp_coef, obs_cells, obs_levels, obs_bary, obs_vfrac, obs_values, obs_mask):
    coef = hyper_coef[:, None, None]
    damp = damp_coef[:, None, None]
    divergence = diff_x(wind_u) + diff_y(wind_v)
    theta_next = theta_field - coef * laplace(laplace(theta_field)) - 0.5 * (wind_u * diff_x(theta_field) + wind_v * diff_y(theta_field))
    wind_u_next = wind_u - coef * laplace(laplace(wind_u)) + damp * diff_x(divergence)
    wind_v_next = wind_v - coef * laplace(laplace(wind_v)) + damp * diff_y(divergence)
    dest = jnp.arange(PATCHES, dtype=jnp.int32)[None, :, None]
    row_base = (dest // N_PY) * CX + obs_cells // CY
    col_base = (dest % N_PY) * CY + obs_cells % CY
    plane = NX * NY
    base = obs_levels * plane + row_base * NY + col_base
    flat = theta_next.reshape(-1)
    above = obs_vfrac
    model = jnp.zeros(obs_values.shape, jnp.float32)
    for index, offset in enumerate((0, NY, 1)):
        cell_id = (base + offset).astype(jnp.int32)
        column = (1.0 - above) * flat[cell_id] + above * flat[cell_id + plane]
        model = model + obs_bary[:, :, index, :] * column
    departures = obs_mask.astype(jnp.float32) * (obs_values - model)
    return theta_next, wind_u_next, wind_v_next, departures
```

```python
import functools

import jax
import jax.numpy as jnp
from jax import lax
from jax.experimental import pallas as pl
from jax.experimental.pallas import tpu as pltpu
from jax.sharding import PartitionSpec as P

LEV = 32
CX = 16
CY = 128
RING = 24
FIELDS = 3
SENT = 5
BOTH = ("px", "py")
F32 = jnp.float32
VMEM = pl.BlockSpec(memory_space=pltpu.VMEM)


def call(kernel, outs, scratch=(), flops=1000, moved=1000):
    return pl.pallas_call(
        kernel,
        out_shape=outs,
        scratch_shapes=scratch,
        compiler_params=pltpu.CompilerParams(vmem_limit_bytes=48 << 20),
        cost_estimate=pl.CostEstimate(flops=flops, bytes_accessed=moved, transcendentals=0),
    )


def pack_obs(cells, levels, bary, vfrac, out):
    rows = cells.shape[0]
    parts = (
        cells[...].astype(F32),
        levels[...].astype(F32),
        vfrac[...],
        bary[:, 0, :],
        bary[:, 1, :],
    )
    for k, part in enumerate(parts):
        out[pl.ds(k, rows, stride=SENT), :] = part


def pack_rows(u, v, t, low, high):
    for f, field in enumerate((u, v, t)):
        for i in range(2):
            at = (i * FIELDS + f) * LEV
            low[at : at + LEV, :] = field[pl.ds(i, LEV, stride=CX), :]
            high[at : at + LEV, :] = field[pl.ds(CX - 2 + i, LEV, stride=CX), :]


def pack_columns(u, v, t, above, below, ring, first, last):
    for f, field in enumerate((u, v, t)):
        for i in range(2):
            at = (i * FIELDS + f) * LEV
            ring[pl.ds(f * LEV * RING + CX + i, LEV, stride=RING), :] = below[at : at + LEV, :]
            ring[pl.ds(f * LEV * RING + RING - 2 + i, LEV, stride=RING), :] = above[at : at + LEV, :]
            ring[pl.ds(f * LEV * RING + CX + 2 + i, LEV, stride=RING), :] = jnp.zeros((LEV, CY), F32)
            ring[pl.ds(f * LEV * RING + CX + 4 + i, LEV, stride=RING), :] = jnp.zeros((LEV, CY), F32)
        for lev in range(LEV):
            ring[(f * LEV + lev) * RING : (f * LEV + lev) * RING + CX, :] = field[lev * CX : (lev + 1) * CX, :]
    for k in range(FIELDS * LEV * RING // 128):
        turned = ring[k * 128 : (k + 1) * 128, :].T
        first[2 * k : 2 * k + 2, :] = turned[0:2, :]
        last[2 * k : 2 * k + 2, :] = turned[CY - 2 :, :]


def step(ring, east, west, hyper, damp, u_out, v_out, t_out, table, side, turn):
    turn[...] = jnp.zeros_like(turn)
    for k in range(FIELDS * LEV * RING // 128):
        turn[0:2, :] = east[2 * k : 2 * k + 2, :]
        turn[CY - 2 :, :] = west[2 * k : 2 * k + 2, :]
        side[k * 128 : (k + 1) * 128, :] = turn[...].T
    lane = lax.broadcasted_iota(jnp.int32, (RING, CY), 1)

    def shifted(field, border, b):
        if b > 0:
            return pltpu.roll(jnp.where(lane < b, border, field), CY - b, 1)
        return pltpu.roll(jnp.where(lane >= CY + b, border, field), -b, 1)

    def rows(value, a):
        return pltpu.roll(value, (RING - a) % RING, 0)[:CX, :]

    def level(lev, carry):
        coef = hyper[lev]
        quarter = damp[lev] * 0.25
        views = []
        fourth = []
        for f in range(FIELDS):
            at = pl.multiple_of((f * LEV + lev) * RING, 8)
            c = ring[pl.ds(at, RING), :]
            h = side[pl.ds(at, RING), :]
            e1, e2, w1, w2 = (shifted(c, h, b) for b in (1, 2, -1, -2))
            r0 = (42.0 * c - 10.0 * (e1 + w1) + (e2 + w2))[:CX, :]
            up1 = 2.0 * (e1 + w2) - 10.0 * (c + w1)
            dn1 = 2.0 * (w1 + e2) - 10.0 * (c + e1)
            up2 = c + w2 + 2.0 * w1
            dn2 = c + e2 + 2.0 * e1
            fourth.append(r0 + rows(up1, 1) + rows(dn1, -1) + rows(up2, 2) + rows(dn2, -2))
            views.append((c, e1, w1, e2, w2))
        (u, ue, uw, _, _), (v, ve, vw, ve2, vw2), (t, te, tw, _, _) = views
        u0, v0, t0 = u[:CX, :], v[:CX, :], t[:CX, :]
        du, dv = ue - uw, ve - vw
        uxx = rows(u, 2) - 2.0 * u0 + rows(u, -2)
        vxy = rows(dv, 1) - rows(dv, -1)
        uxy = rows(du, 1) - rows(du, -1)
        vyy = ve2[:CX, :] - 2.0 * v0 + vw2[:CX, :]
        out_at = pl.multiple_of(lev * CX, 8)
        u_out[pl.ds(out_at, CX), :] = u0 - coef * fourth[0] + quarter * (uxx + vxy)
        v_out[pl.ds(out_at, CX), :] = v0 - coef * fourth[1] + quarter * (uxy + vyy)
        t_out[pl.ds(out_at, CX), :] = (
            t0
            - coef * fourth[2]
            - 0.25 * (u0 * (rows(t, 1) - rows(t, -1)) + v0 * (te - tw)[:CX, :])
        )
        return carry

    lax.fori_loop(0, LEV, level, 0)
    for r in range(CX):
        here = t_out[pl.ds(r, LEV, stride=CX), :]
        for s, part in enumerate((here, pltpu.roll(here, CY - 1, 1))):
            high = part.astype(jnp.bfloat16)
            low = (part - high.astype(F32)).astype(jnp.bfloat16)
            at = (s * CX + r) * LEV
            table[at : at + LEV, :CY] = high
            table[at : at + LEV, CY:] = low


def interpolate(table, obs, model, col, row, lev, fra, b0, b1):
    owners = model.shape[0]
    cell = obs[pl.ds(0, owners, stride=SENT), :].astype(jnp.int32)
    col[...] = cell & (CY - 1)
    row[...] = cell >> 7
    lev[...] = obs[pl.ds(1, owners, stride=SENT), :].astype(jnp.int32)
    fra[...] = obs[pl.ds(2, owners, stride=SENT), :]
    b0[...] = obs[pl.ds(3, owners, stride=SENT), :]
    b1[...] = obs[pl.ds(4, owners, stride=SENT), :]
    cell_iota = lax.broadcasted_iota(jnp.int32, (CY, 256), 0)
    lev_iota = lax.broadcasted_iota(jnp.int32, (LEV, 256), 0)

    def pair(p, carry):
        def two(ref):
            return jnp.concatenate([ref[pl.ds(2 * p, 1), :], ref[pl.ds(2 * p + 1, 1), :]], axis=1)

        c, r, l, a, w0, w1 = (two(ref) for ref in (col, row, lev, fra, b0, b1))
        w2 = 1.0 - w0 - w1
        hot = jnp.where(cell_iota == c, 1.0, 0.0).astype(jnp.bfloat16)
        hot = jnp.concatenate([hot, hot], axis=0)
        got = jnp.dot(table[...], hot, preferred_element_type=F32)
        total = jnp.zeros((LEV, 256), F32)
        for i in range(CX):
            here = jnp.where(r == i, w0, jnp.where(r == i - 1, w1, 0.0))
            total = total + here * got[i * LEV : (i + 1) * LEV, :]
            if i < CX - 1:
                beside = jnp.where(r == i, w2, 0.0)
                total = total + beside * got[(CX + i) * LEV : (CX + i + 1) * LEV, :]
        weight = jnp.where(lev_iota == l, 1.0 - a, jnp.where(lev_iota == l + 1, a, 0.0))
        out = jnp.sum(weight * total, axis=0, keepdims=True)
        model[pl.ds(2 * p, 1), :] = out[:, :128]
        model[pl.ds(2 * p + 1, 1), :] = out[:, 128:]
        return carry

    lax.fori_loop(0, owners // 2, pair, 0)


def neighbour(axis, move):
    count = lax.axis_size(axis)
    return [(i, (i + move) % count) for i in range(count)]


def on_device(theta, wind_u, wind_v, hyper, damp, cells, levels, bary, vfrac, values, mask):
    flat = LEV * CX
    fields = tuple(f.reshape(flat, CY) for f in (wind_u, wind_v, theta))
    owners, slots = cells.shape[1], cells.shape[2]
    shape = jax.ShapeDtypeStruct
    edge = shape((2 * FIELDS * LEV, CY), F32)
    low, high = call(pack_rows, (edge, edge))(*fields)
    sent = call(pack_obs, shape((owners * SENT, slots), F32))(
        cells[0], levels[0], bary[0], vfrac[0]
    )
    above = lax.ppermute(high, "px", neighbour("px", 1))
    below = lax.ppermute(low, "px", neighbour("px", -1))
    got = lax.all_to_all(sent, BOTH, split_axis=0, concat_axis=0, tiled=True)
    ring_rows = FIELDS * LEV * RING
    side = shape((ring_rows // 64, CY), F32)
    ring, first, last = call(pack_columns, (shape((ring_rows, CY), F32), side, side))(
        *fields, above, below
    )
    west = lax.ppermute(last, "py", neighbour("py", 1))
    east = lax.ppermute(first, "py", neighbour("py", -1))
    patch = shape((flat, CY), F32)
    smem = pl.BlockSpec(memory_space=pltpu.SMEM)
    u_next, v_next, t_next, table = pl.pallas_call(
        step,
        out_shape=(patch, patch, patch, shape((2 * flat, 2 * CY), jnp.bfloat16)),
        in_specs=[VMEM, VMEM, VMEM, smem, smem],
        scratch_shapes=[pltpu.VMEM((ring_rows, CY), F32), pltpu.VMEM((CY, CY), F32)],
        compiler_params=pltpu.CompilerParams(vmem_limit_bytes=48 << 20),
        cost_estimate=pl.CostEstimate(flops=4000000, bytes_accessed=4000000, transcendentals=0),
    )(ring, east, west, hyper, damp)
    ints = pltpu.VMEM((owners, slots), jnp.int32)
    floats = pltpu.VMEM((owners, slots), F32)
    model = call(
        interpolate,
        shape((owners, slots), F32),
        scratch=[ints, ints, ints, floats, floats, floats],
        flops=8000000000,
        moved=1000000,
    )(table, got)
    back = lax.all_to_all(model, BOTH, split_axis=0, concat_axis=0, tiled=True)
    departures = mask.astype(F32) * (values - back[None])
    whole = theta.shape
    return t_next.reshape(whole), u_next.reshape(whole), v_next.reshape(whole), departures


def solution(mesh):
    field = P(None, "px", "py")
    obs = P(BOTH, None, None)
    return jax.shard_map(
        on_device,
        mesh=mesh,
        in_specs=(field, field, field, P(), P(), obs, obs, P(BOTH, None, None, None), obs, obs, obs),
        out_specs=(field, field, field, obs),
        check_vma=False,
    )
```

```python
import jax
import jax.numpy as jnp
from jax import lax
from jax.experimental import pallas as pl
from jax.experimental.pallas import tpu as pltpu
from jax.sharding import PartitionSpec as P

LEV = 32
CX = 16
CY = 128
FLAT = LEV * CX
FIELDS = 3
OBS = 5
SENT = OBS + FIELDS
ROWS = (0, 1, CX - 2, CX - 1)
BLOCKS = FIELDS * FLAT // 128
EDGE = 2 * FIELDS * LEV
UNROLL = 16
BOTH = ("px", "py")
F32 = jnp.float32
BF16 = jnp.bfloat16
VMEM = pl.BlockSpec(memory_space=pltpu.VMEM)
SMEM = pl.BlockSpec(memory_space=pltpu.SMEM)
HBM = pl.BlockSpec(memory_space=pltpu.MemorySpace.HBM)
PARAMS = pltpu.CompilerParams(vmem_limit_bytes=48 << 20)


WHOLE = pltpu.CompilerParams(vmem_limit_bytes=60 << 20)


def cost(flops, moved):
    return pl.CostEstimate(flops=flops, bytes_accessed=moved, transcendentals=0)


def diagonal(move_x, move_y):
    count_x, count_y = lax.axis_size("px"), lax.axis_size("py")
    x = lax.rem(lax.axis_index("px") + count_x + move_x, count_x)
    return x * count_y + lax.rem(lax.axis_index("py") + count_y + move_y, count_y)


def messages_out(u, v, t, cells, levels, bary, vfrac, sent, fields, ints, floats, weights, packed, turn, sems):
    copies = [
        pltpu.make_async_copy(u, fields.at[0], sems.at[0]),
        pltpu.make_async_copy(v, fields.at[1], sems.at[1]),
        pltpu.make_async_copy(t, fields.at[2], sems.at[2]),
        pltpu.make_async_copy(cells, ints.at[0], sems.at[3]),
        pltpu.make_async_copy(levels, ints.at[1], sems.at[4]),
        pltpu.make_async_copy(vfrac, floats, sems.at[5]),
        pltpu.make_async_copy(bary.at[pl.ds(0, 2)], weights, sems.at[6]),
    ]
    for copy in copies:
        copy.start()
    packed[:, OBS:, :] = jnp.zeros((packed.shape[0], FIELDS, CY), F32)
    for copy in copies:
        copy.wait()
    packed[:, 0, :] = ints[0].astype(F32)
    packed[:, 1, :] = ints[1].astype(F32)
    packed[:, 2, :] = floats[...]
    packed[:, 3, :] = weights[0]
    packed[:, 4, :] = weights[1]
    half = lax.broadcasted_iota(jnp.int32, (1, CY), 1) < CY // 2
    for f in range(FIELDS):
        for i, r in enumerate(ROWS):
            turn[i * LEV : (i + 1) * LEV, :] = fields[f, pl.ds(r, LEV, stride=CX), :]
        turned = turn[...].T
        for move_y, c in ((-1, 0), (1, CY - 2)):
            one, two = turned[c : c + 1, :], turned[c + 1 : c + 2, :]
            row = OBS + f
            packed[diagonal(-1, move_y), row : row + 1, :] = jnp.where(
                half, one, pltpu.roll(two, CY // 2, 1)
            )
            packed[diagonal(1, move_y), row : row + 1, :] = jnp.where(
                half, pltpu.roll(one, CY // 2, 1), two
            )
    pltpu.sync_copy(packed, sent)


def edges_out(u, v, t, first, last, low, high):
    for f, field in enumerate((u, v, t)):
        for i in range(2):
            at = (i * FIELDS + f) * LEV
            low[at : at + LEV, :] = field[pl.ds(i, LEV, stride=CX), :]
            high[at : at + LEV, :] = field[pl.ds(CX - 2 + i, LEV, stride=CX), :]
        for k in range(FLAT // 128):
            turned = field[k * 128 : (k + 1) * 128, :].T
            at = 2 * (f * FLAT // 128 + k)
            first[at : at + 2, :] = turned[0:2, :]
            last[at : at + 2, :] = turned[CY - 2 :, :]


def shifted(lane, field, border, b):
    if b > 0:
        return pltpu.roll(jnp.where(lane < b, border, field), CY - b, 1)
    return pltpu.roll(jnp.where(lane >= CY + b, border, field), -b, 1)


def spread(turn, ahead, behind):
    turn[0:2, :] = ahead
    turn[CY - 2 :, :] = behind
    return turn[...].T


def inner(u, v, t, east, west, hyper, damp, u_out, v_out, t_out, pick, side, turn):
    turn[...] = jnp.zeros_like(turn)
    for k in range(BLOCKS):
        side[k * 128 : (k + 1) * 128, :] = spread(
            turn, east[2 * k : 2 * k + 2, :], west[2 * k : 2 * k + 2, :]
        )
    lane = lax.broadcasted_iota(jnp.int32, (CX, CY), 1)
    none = jnp.zeros((8, CY), F32)

    def rows(value, a):
        return pltpu.roll(jnp.concatenate([value, none], axis=0), -a % (CX + 8), 0)[:CX, :]

    def level(lev, carry):
        coef = hyper[lev]
        quarter = damp[lev] * 0.25
        at = pl.multiple_of(lev * CX, 8)
        views = []
        fourth = []
        for f, field in enumerate((u, v, t)):
            c = field[pl.ds(at, CX), :]
            h = side[pl.ds(f * FLAT + at, CX), :]
            e1, e2, w1, w2 = (shifted(lane, c, h, b) for b in (1, 2, -1, -2))
            total = 42.0 * c - 10.0 * (e1 + w1) + (e2 + w2)
            total = total + rows(2.0 * (e1 + w2) - 10.0 * (c + w1), 1)
            total = total + rows(2.0 * (w1 + e2) - 10.0 * (c + e1), -1)
            total = total + rows(c + w2 + 2.0 * w1, 2) + rows(c + e2 + 2.0 * e1, -2)
            fourth.append(total)
            views.append((c, e1, w1, e2, w2))
        (u0, ue, uw, _, _), (v0, ve, vw, ve2, vw2), (t0, te, tw, _, _) = views
        du, dv = ue - uw, ve - vw
        uxx = rows(u0, 2) - 2.0 * u0 + rows(u0, -2)
        vxy = rows(dv, 1) - rows(dv, -1)
        uxy = rows(du, 1) - rows(du, -1)
        vyy = ve2 - 2.0 * v0 + vw2
        u_out[pl.ds(at, CX), :] = u0 - coef * fourth[0] + quarter * (uxx + vxy)
        v_out[pl.ds(at, CX), :] = v0 - coef * fourth[1] + quarter * (uxy + vyy)
        drift = u0 * (rows(t0, 1) - rows(t0, -1)) + v0 * (te - tw)
        t_out[pl.ds(at, CX), :] = t0 - coef * fourth[2] - 0.25 * drift
        return carry

    lax.fori_loop(0, LEV, level, 0, unroll=4)
    k = lax.broadcasted_iota(jnp.int32, pick.shape, 0)
    n = lax.broadcasted_iota(jnp.int32, pick.shape, 1)
    want = ((n >> 5) & 3) * CY + (n & 31) * 4 + (n >> 7)
    pick[...] = jnp.where(k == want, 1.0, 0.0).astype(BF16)


def per_level(coef, quarter, hyper, damp):
    for lev in range(LEV):
        coef[lev : lev + 1, :] = jnp.full((1, CY), hyper[lev], F32)
        quarter[lev : lev + 1, :] = jnp.full((1, CY), damp[lev] * 0.25, F32)


def one(line, sign):
    c, e1, e2, w1, w2 = line
    if sign > 0:
        return 2.0 * (e1 + w2) - 10.0 * (c + w1)
    return 2.0 * (w1 + e2) - 10.0 * (c + e1)


def two(line, sign):
    c, e1, e2, w1, w2 = line
    return c + w2 + 2.0 * w1 if sign > 0 else c + e2 + 2.0 * e1


def add(out, r, value):
    out[pl.ds(r, LEV, stride=CX), :] += value


def add_rows(u_out, v_out, t_out, near, far, sign, k4, k2, wind):
    edge, following = (CX - 1, CX - 2) if sign > 0 else (0, 1)
    cross = [line[1] - line[3] for line in near]
    fourth = [one(near[f], sign) + two(far[f], sign) for f in range(FIELDS)]
    add(u_out, edge, k2 * (far[0][0] + sign * cross[1]) - k4 * fourth[0])
    add(u_out, following, k2 * near[0][0] - k4 * two(near[0], sign))
    add(v_out, edge, k2 * (sign * cross[0]) - k4 * fourth[1])
    add(v_out, following, -k4 * two(near[1], sign))
    add(t_out, edge, -k4 * fourth[2] - (0.25 * sign) * wind * near[2][0])
    add(t_out, following, -k4 * two(near[2], sign))


def finish(u, u_in, v_in, t_in, above, below, hyper, damp, pick, u_out, v_out, t_out, table, coef, quarter):
    per_level(coef, quarter, hyper, damp)
    u_out[...] = u_in[...]
    v_out[...] = v_in[...]
    t_out[...] = t_in[...]
    lane = lax.broadcasted_iota(jnp.int32, (LEV, CY), 1)
    none = jnp.zeros((LEV, CY), F32)

    def outside(rows, i):
        line = []
        for f in range(FIELDS):
            c = rows[(i * FIELDS + f) * LEV : (i * FIELDS + f + 1) * LEV, :]
            line.append((c,) + tuple(shifted(lane, c, none, b) for b in (1, 2, -1, -2)))
        return line

    for sign, rows, near, far in ((-1, above, 1, 0), (1, below, 0, 1)):
        wind = u[pl.ds(0 if sign < 0 else CX - 1, LEV, stride=CX), :]
        add_rows(
            u_out, v_out, t_out, outside(rows, near), outside(rows, far), sign, coef[...], quarter[...], wind
        )
    for rl in range(4):
        parts = [t_out[pl.ds(4 * rh + rl, LEV, stride=CX), :] for rh in range(4)]
        tops = [part.astype(BF16) for part in parts]
        rests = [(part - top.astype(F32)).astype(BF16) for part, top in zip(parts, tops)]
        both = jnp.concatenate(
            [jnp.concatenate(tops, axis=1), jnp.concatenate(rests, axis=1)], axis=0
        )
        put = jnp.dot(both, pick[...], preferred_element_type=F32)
        for half in range(2):
            lanes = slice(half * 128, half * 128 + 128)
            for cl in range(4):
                x = put[half * LEV : (half + 1) * LEV, cl * 128 : (cl + 1) * 128]
                table[(rl * 5 + cl) * LEV : (rl * 5 + cl + 1) * LEV, lanes] = x.astype(BF16)
                if cl == 0:
                    table[(rl * 5 + 4) * LEV : (rl * 5 + 5) * LEV, lanes] = pltpu.roll(
                        x, 127, 1
                    ).astype(BF16)
                if rl == 0:
                    table[(20 + cl) * LEV : (21 + cl) * LEV, lanes] = pltpu.roll(x, 96, 1).astype(BF16)


def corner_lines(obs, turn, f):
    turn[...] = jnp.zeros_like(turn)
    row = OBS + f
    half = lax.broadcasted_iota(jnp.int32, (1, CY), 1) < CY // 2
    for move_y, c in ((1, 0), (-1, CY - 2)):
        upper = obs[diagonal(-1, move_y), row : row + 1, :]
        lower = obs[diagonal(1, move_y), row : row + 1, :]
        turn[c : c + 1, :] = jnp.where(half, upper, pltpu.roll(lower, CY // 2, 1))
        turn[c + 1 : c + 2, :] = jnp.where(half, pltpu.roll(upper, CY // 2, 1), lower)
    spots = turn[...].T
    lane = lax.broadcasted_iota(jnp.int32, (LEV, CY), 1)
    none = jnp.zeros((LEV, CY), F32)
    lines = []
    for i in range(4):
        h = spots[i * LEV : (i + 1) * LEV, :]
        lines.append((none,) + tuple(shifted(lane, none, h, b) for b in (1, 2, -1, -2)))
    return lines


def corners(obs, u_in, v_in, t_in, hyper, damp, u_out, v_out, t_out, turn, coef, quarter):
    per_level(coef, quarter, hyper, damp)
    u_out[...] = u_in[...]
    v_out[...] = v_in[...]
    t_out[...] = t_in[...]
    lines = [corner_lines(obs, turn, f) for f in range(FIELDS)]
    none = jnp.zeros((LEV, CY), F32)
    for sign, near, far in ((-1, 1, 0), (1, 2, 3)):
        add_rows(
            u_out,
            v_out,
            t_out,
            [line[near] for line in lines],
            [line[far] for line in lines],
            sign,
            coef[...],
            quarter[...],
            none,
        )


def interpolate(start, obs, t, hyper, model, table, block, row, col, lev, turn, coef):
    table[...] = start[...]
    for k in range(LEV):
        coef[k : k + 1, :] = jnp.full((1, CY), hyper[k], F32)
    far_up, near_up, near_down, far_down = corner_lines(obs, turn, 2)
    terms = (
        one(near_up, -1) + two(far_up, -1),
        two(near_up, -1),
        two(near_down, 1),
        one(near_down, 1) + two(far_down, 1),
    )
    lane = lax.broadcasted_iota(jnp.int32, (LEV, CY), 1)
    for r, term in zip(ROWS, terms):
        value = t[pl.ds(r, LEV, stride=CX), :] - coef[...] * term
        for c in (0, 1, CY - 2, CY - 1):
            to = (r >> 2) * 32 + (c >> 2)
            moved = pltpu.roll(value, (to - c) % CY, 1)
            high = moved.astype(BF16).astype(F32)
            at = ((r & 3) * 5 + (c & 3)) * LEV
            for k, part in enumerate((high, moved - high)):
                old = table[at : at + LEV, k * CY : (k + 1) * CY].astype(F32)
                table[at : at + LEV, k * CY : (k + 1) * CY] = jnp.where(lane == to, part, old).astype(BF16)
    owners = model.shape[0]
    cell = obs[:, 0, :].astype(jnp.int32)
    c, r = cell & (CY - 1), cell >> 7
    block[...] = (r >> 2) * 32 + (c >> 2)
    row[...] = r & 3
    col[...] = c & 3
    lev[...] = obs[:, 1, :].astype(jnp.int32)
    wide = 256
    block_iota = lax.broadcasted_iota(jnp.int32, (128, wide), 0)
    lev_iota = lax.broadcasted_iota(jnp.int32, (LEV, wide), 0)

    def pair(p, carry):
        def two(ref):
            return jnp.concatenate([ref[pl.ds(2 * p, 1), :], ref[pl.ds(2 * p + 1, 1), :]], axis=1)

        def sent(k):
            return jnp.concatenate([obs[2 * p, k : k + 1, :], obs[2 * p + 1, k : k + 1, :]], axis=1)

        def bit(value, mask):
            return jnp.broadcast_to(value & mask, (LEV, wide)) != 0

        at, r, c, l = two(block), two(row), two(col), two(lev)
        a, w0, w1 = sent(2), sent(3), sent(4)
        w2 = 1.0 - w0 - w1
        hot = jnp.where(block_iota == at, 1.0, 0.0).astype(BF16)
        got = jnp.dot(
            table[...], jnp.concatenate([hot, hot], axis=0), preferred_element_type=F32
        )
        c1, c2, r1, r2 = bit(c, 1), bit(c, 2), bit(r, 1), bit(r, 2)
        here, beside = [], []
        for i in range(5):
            g = [got[(i * 5 + j) * LEV : (i * 5 + j + 1) * LEV, :] for j in range(5 if i < 4 else 4)]
            h1 = jnp.where(c2, g[3], g[1])
            here.append(jnp.where(c1, h1, jnp.where(c2, g[2], g[0])))
            if i < 4:
                beside.append(jnp.where(c1, jnp.where(c2, g[4], g[2]), h1))
        h0, h1, h2 = (jnp.where(r2, here[i + 2], here[i]) for i in range(3))
        t0, t1 = jnp.where(r1, h1, h0), jnp.where(r1, h2, h1)
        t2 = jnp.where(
            r1, jnp.where(r2, beside[3], beside[1]), jnp.where(r2, beside[2], beside[0])
        )
        weight = jnp.where(lev_iota == l, 1.0 - a, jnp.where(lev_iota == l + 1, a, 0.0))
        out = jnp.sum(weight * (w0 * t0 + w1 * t1 + w2 * t2), axis=0, keepdims=True)
        model[pl.ds(2 * p, 1), :] = out[:, :128]
        model[pl.ds(2 * p + 1, 1), :] = out[:, 128:]
        return carry

    lax.fori_loop(0, owners // 2, pair, 0, unroll=UNROLL)


def neighbour(axis, move):
    count = lax.axis_size(axis)
    return [(i, (i + move) % count) for i in range(count)]


def on_device(theta, wind_u, wind_v, hyper, damp, cells, levels, bary, vfrac, values, mask):
    u, v, t = (f.reshape(FLAT, CY) for f in (wind_u, wind_v, theta))
    owners, slots = cells.shape[1], cells.shape[2]
    shape = jax.ShapeDtypeStruct
    sent = pl.pallas_call(
        messages_out,
        out_shape=shape((owners, SENT, slots), F32),
        in_specs=[HBM] * 7,
        out_specs=HBM,
        scratch_shapes=[
            pltpu.VMEM((FIELDS, FLAT, CY), F32),
            pltpu.VMEM((2, owners, slots), jnp.int32),
            pltpu.VMEM((owners, slots), F32),
            pltpu.VMEM((2, owners, slots), F32),
            pltpu.VMEM((owners, SENT, slots), F32),
            pltpu.VMEM((CY, CY), F32),
            pltpu.SemaphoreType.DMA((7,)),
        ],
        compiler_params=WHOLE,
        cost_estimate=cost(100000, 3000000),
    )(u, v, t, cells[0], levels[0], jnp.swapaxes(bary[0], 0, 1), vfrac[0])
    got = lax.all_to_all(sent, BOTH, split_axis=0, concat_axis=0, tiled=True)
    columns = shape((2 * BLOCKS, CY), F32)
    edge = shape((EDGE, CY), F32)
    first, last, low, high = pl.pallas_call(
        edges_out,
        out_shape=(columns, columns, edge, edge),
        in_specs=[VMEM] * 3,
        compiler_params=PARAMS,
        cost_estimate=cost(100000, 1000000),
    )(u, v, t)
    west = lax.ppermute(last, "py", neighbour("py", 1))
    east = lax.ppermute(first, "py", neighbour("py", -1))
    above = lax.ppermute(high, "px", neighbour("px", 1))
    below = lax.ppermute(low, "px", neighbour("px", -1))
    patch = shape((FLAT, CY), F32)
    turn = pltpu.VMEM((CY, CY), F32)
    each = pltpu.VMEM((LEV, CY), F32)
    u_part, v_part, t_part, pick = pl.pallas_call(
        inner,
        out_shape=(patch, patch, patch, shape((4 * CY, 4 * CY), BF16)),
        in_specs=[VMEM] * 5 + [SMEM] * 2,
        scratch_shapes=[pltpu.VMEM((FIELDS * FLAT, CY), F32), turn],
        compiler_params=PARAMS,
        cost_estimate=cost(8000000, 3000000),
    )(u, v, t, east, west, hyper, damp)
    u_most, v_most, t_most, table = pl.pallas_call(
        finish,
        out_shape=(patch, patch, patch, shape((24 * LEV, 2 * CY), BF16)),
        in_specs=[VMEM] * 6 + [SMEM] * 2 + [VMEM],
        scratch_shapes=[each, each],
        compiler_params=PARAMS,
        cost_estimate=cost(4000000, 3000000),
    )(u, u_part, v_part, t_part, above, below, hyper, damp, pick)
    model = pl.pallas_call(
        interpolate,
        out_shape=shape((owners, slots), F32),
        in_specs=[VMEM] * 3 + [SMEM],
        scratch_shapes=[pltpu.VMEM((24 * LEV, 2 * CY), BF16)]
        + [pltpu.VMEM((owners, slots), jnp.int32)] * 4
        + [turn, each],
        compiler_params=PARAMS,
        cost_estimate=cost(6500000000, 1000000),
    )(table, got, t_most, hyper)
    u_next, v_next, t_next = pl.pallas_call(
        corners,
        out_shape=(patch, patch, patch),
        in_specs=[VMEM] * 4 + [SMEM] * 2,
        scratch_shapes=[turn, each, each],
        compiler_params=PARAMS,
        cost_estimate=cost(4000000, 3000000),
    )(got, u_most, v_most, t_most, hyper, damp)
    back = lax.all_to_all(model, BOTH, split_axis=0, concat_axis=0, tiled=True)
    departures = mask.astype(F32) * (values - back[None])
    whole = theta.shape
    return t_next.reshape(whole), u_next.reshape(whole), v_next.reshape(whole), departures


def solution(mesh):
    field = P(None, "px", "py")
    obs = P(BOTH, None, None)
    return jax.shard_map(
        on_device,
        mesh=mesh,
        in_specs=(field, field, field, P(), P(), obs, obs, P(BOTH, None, None, None), obs, obs, obs),
        out_specs=(field, field, field, obs),
        check_vma=False,
    )
```

```python
import jax
import jax.numpy as jnp
from jax import lax
from jax.experimental import pallas as pl
from jax.experimental.pallas import tpu as pltpu
from jax.sharding import PartitionSpec as P

LEV = 32
CX = 16
CY = 128
FLAT = LEV * CX
FIELDS = 3
OBS = 5
SENT = OBS + FIELDS
ROWS = (0, 1, CX - 2, CX - 1)
BLOCKS = FIELDS * FLAT // 128
EDGE = 2 * FIELDS * LEV
UNROLL = 16
BOTH = ("px", "py")
F32 = jnp.float32
BF16 = jnp.bfloat16
VMEM = pl.BlockSpec(memory_space=pltpu.VMEM)
SMEM = pl.BlockSpec(memory_space=pltpu.SMEM)
HBM = pl.BlockSpec(memory_space=pltpu.MemorySpace.HBM)
PARAMS = pltpu.CompilerParams(vmem_limit_bytes=48 << 20)


WHOLE = pltpu.CompilerParams(vmem_limit_bytes=60 << 20)


def cost(flops, moved):
    return pl.CostEstimate(flops=flops, bytes_accessed=moved, transcendentals=0)


def diagonal(move_x, move_y):
    count_x, count_y = lax.axis_size("px"), lax.axis_size("py")
    x = lax.rem(lax.axis_index("px") + count_x + move_x, count_x)
    return x * count_y + lax.rem(lax.axis_index("py") + count_y + move_y, count_y)


def messages_out(u, v, t, cells, levels, bary, vfrac, sent, fields, ints, floats, weights, packed, turn, sems):
    copies = [
        pltpu.make_async_copy(u, fields.at[0], sems.at[0]),
        pltpu.make_async_copy(v, fields.at[1], sems.at[1]),
        pltpu.make_async_copy(t, fields.at[2], sems.at[2]),
        pltpu.make_async_copy(cells, ints.at[0], sems.at[3]),
        pltpu.make_async_copy(levels, ints.at[1], sems.at[4]),
        pltpu.make_async_copy(vfrac, floats, sems.at[5]),
        pltpu.make_async_copy(bary.at[pl.ds(0, 2)], weights, sems.at[6]),
    ]
    for copy in copies:
        copy.start()
    packed[:, OBS:, :] = jnp.zeros((packed.shape[0], FIELDS, CY), F32)
    for copy in copies:
        copy.wait()
    packed[:, 0, :] = ints[0].astype(F32)
    packed[:, 1, :] = ints[1].astype(F32)
    packed[:, 2, :] = floats[...]
    packed[:, 3, :] = weights[0]
    packed[:, 4, :] = weights[1]
    half = lax.broadcasted_iota(jnp.int32, (1, CY), 1) < CY // 2
    for f in range(FIELDS):
        for i, r in enumerate(ROWS):
            turn[i * LEV : (i + 1) * LEV, :] = fields[f, pl.ds(r, LEV, stride=CX), :]
        turned = turn[...].T
        for move_y, c in ((-1, 0), (1, CY - 2)):
            one, two = turned[c : c + 1, :], turned[c + 1 : c + 2, :]
            row = OBS + f
            packed[diagonal(-1, move_y), row : row + 1, :] = jnp.where(
                half, one, pltpu.roll(two, CY // 2, 1)
            )
            packed[diagonal(1, move_y), row : row + 1, :] = jnp.where(
                half, pltpu.roll(one, CY // 2, 1), two
            )
    pltpu.sync_copy(packed, sent)


def is_even(axis):
    return lax.rem(lax.axis_index(axis), 2) == 0


def edges_out(u, v, t, col_a, col_b, row_a, row_b):
    even_x, even_y = is_even("px"), is_even("py")
    for f, field in enumerate((u, v, t)):
        for i in range(2):
            at = (i * FIELDS + f) * LEV
            low = field[pl.ds(i, LEV, stride=CX), :]
            high = field[pl.ds(CX - 2 + i, LEV, stride=CX), :]
            row_a[at : at + LEV, :] = jnp.where(even_x, high, low)
            row_b[at : at + LEV, :] = jnp.where(even_x, low, high)
        for k in range(FLAT // 128):
            turned = field[k * 128 : (k + 1) * 128, :].T
            first, last = turned[0:2, :], turned[CY - 2 :, :]
            at = 2 * (f * FLAT // 128 + k)
            col_a[at : at + 2, :] = jnp.where(even_y, last, first)
            col_b[at : at + 2, :] = jnp.where(even_y, first, last)


def selector(pick):
    k = lax.broadcasted_iota(jnp.int32, pick.shape, 0)
    n = lax.broadcasted_iota(jnp.int32, pick.shape, 1)
    want = ((n >> 5) & 3) * CY + (n & 31) * 4 + (n >> 7)
    pick[...] = jnp.where(k == want, 1.0, 0.0).astype(BF16)


def shifted(lane, field, border, b):
    if b > 0:
        return pltpu.roll(jnp.where(lane < b, border, field), CY - b, 1)
    return pltpu.roll(jnp.where(lane >= CY + b, border, field), -b, 1)


def spread(turn, ahead, behind):
    turn[0:2, :] = ahead
    turn[CY - 2 :, :] = behind
    return turn[...].T


def per_level(coef, quarter, hyper, damp):
    for lev in range(LEV):
        coef[lev : lev + 1, :] = jnp.full((1, CY), hyper[lev], F32)
        quarter[lev : lev + 1, :] = jnp.full((1, CY), damp[lev] * 0.25, F32)


def one(line, sign):
    c, e1, e2, w1, w2 = line
    if sign > 0:
        return 2.0 * (e1 + w2) - 10.0 * (c + w1)
    return 2.0 * (w1 + e2) - 10.0 * (c + e1)


def two(line, sign):
    c, e1, e2, w1, w2 = line
    return c + w2 + 2.0 * w1 if sign > 0 else c + e2 + 2.0 * e1


def add(out, r, value):
    out[pl.ds(r, LEV, stride=CX), :] += value


def add_rows(u_out, v_out, t_out, near, far, sign, k4, k2, wind):
    edge, following = (CX - 1, CX - 2) if sign > 0 else (0, 1)
    cross = [line[1] - line[3] for line in near]
    fourth = [one(near[f], sign) + two(far[f], sign) for f in range(FIELDS)]
    add(u_out, edge, k2 * (far[0][0] + sign * cross[1]) - k4 * fourth[0])
    add(u_out, following, k2 * near[0][0] - k4 * two(near[0], sign))
    add(v_out, edge, k2 * (sign * cross[0]) - k4 * fourth[1])
    add(v_out, following, -k4 * two(near[1], sign))
    add(t_out, edge, -k4 * fourth[2] - (0.25 * sign) * wind * near[2][0])
    add(t_out, following, -k4 * two(near[2], sign))


def step(u, v, t, col_a, col_b, row_a, row_b, hyper, damp, pick, u_out, v_out, t_out, table, side, turn, coef, quarter):
    even_x, even_y = is_even("px"), is_even("py")
    turn[...] = jnp.zeros_like(turn)
    for k in range(BLOCKS):
        a, b = col_a[2 * k : 2 * k + 2, :], col_b[2 * k : 2 * k + 2, :]
        side[k * 128 : (k + 1) * 128, :] = spread(
            turn, jnp.where(even_y, a, b), jnp.where(even_y, b, a)
        )
    per_level(coef, quarter, hyper, damp)
    lane = lax.broadcasted_iota(jnp.int32, (CX, CY), 1)
    none = jnp.zeros((8, CY), F32)

    def rows(value, a):
        return pltpu.roll(jnp.concatenate([value, none], axis=0), -a % (CX + 8), 0)[:CX, :]

    def level(lev, carry):
        coef = hyper[lev]
        quarter = damp[lev] * 0.25
        at = pl.multiple_of(lev * CX, 8)
        views = []
        fourth = []
        for f, field in enumerate((u, v, t)):
            c = field[pl.ds(at, CX), :]
            h = side[pl.ds(f * FLAT + at, CX), :]
            e1, e2, w1, w2 = (shifted(lane, c, h, b) for b in (1, 2, -1, -2))
            total = 42.0 * c - 10.0 * (e1 + w1) + (e2 + w2)
            total = total + rows(2.0 * (e1 + w2) - 10.0 * (c + w1), 1)
            total = total + rows(2.0 * (w1 + e2) - 10.0 * (c + e1), -1)
            total = total + rows(c + w2 + 2.0 * w1, 2) + rows(c + e2 + 2.0 * e1, -2)
            fourth.append(total)
            views.append((c, e1, w1, e2, w2))
        (u0, ue, uw, _, _), (v0, ve, vw, ve2, vw2), (t0, te, tw, _, _) = views
        du, dv = ue - uw, ve - vw
        uxx = rows(u0, 2) - 2.0 * u0 + rows(u0, -2)
        vxy = rows(dv, 1) - rows(dv, -1)
        uxy = rows(du, 1) - rows(du, -1)
        vyy = ve2 - 2.0 * v0 + vw2
        u_out[pl.ds(at, CX), :] = u0 - coef * fourth[0] + quarter * (uxx + vxy)
        v_out[pl.ds(at, CX), :] = v0 - coef * fourth[1] + quarter * (uxy + vyy)
        drift = u0 * (rows(t0, 1) - rows(t0, -1)) + v0 * (te - tw)
        t_out[pl.ds(at, CX), :] = t0 - coef * fourth[2] - 0.25 * drift
        return carry

    lax.fori_loop(0, LEV, level, 0, unroll=4)
    lane = lax.broadcasted_iota(jnp.int32, (LEV, CY), 1)
    none = jnp.zeros((LEV, CY), F32)

    def outside(this, other, keep, i):
        line = []
        for f in range(FIELDS):
            at = (i * FIELDS + f) * LEV
            c = jnp.where(keep, this[at : at + LEV, :], other[at : at + LEV, :])
            line.append((c,) + tuple(shifted(lane, c, none, b) for b in (1, 2, -1, -2)))
        return line

    for sign, this, other, near, far in ((-1, row_b, row_a, 1, 0), (1, row_a, row_b, 0, 1)):
        wind = u[pl.ds(0 if sign < 0 else CX - 1, LEV, stride=CX), :]
        add_rows(
            u_out,
            v_out,
            t_out,
            outside(this, other, even_x, near),
            outside(this, other, even_x, far),
            sign,
            coef[...],
            quarter[...],
            wind,
        )
    for rl in range(4):
        parts = [t_out[pl.ds(4 * rh + rl, LEV, stride=CX), :] for rh in range(4)]
        tops = [part.astype(BF16) for part in parts]
        rests = [(part - top.astype(F32)).astype(BF16) for part, top in zip(parts, tops)]
        both = jnp.concatenate(
            [jnp.concatenate(tops, axis=1), jnp.concatenate(rests, axis=1)], axis=0
        )
        put = jnp.dot(both, pick[...], preferred_element_type=F32)
        for half in range(2):
            lanes = slice(half * 128, half * 128 + 128)
            for cl in range(4):
                x = put[half * LEV : (half + 1) * LEV, cl * 128 : (cl + 1) * 128]
                table[(rl * 5 + cl) * LEV : (rl * 5 + cl + 1) * LEV, lanes] = x.astype(BF16)
                if cl == 0:
                    table[(rl * 5 + 4) * LEV : (rl * 5 + 5) * LEV, lanes] = pltpu.roll(
                        x, 127, 1
                    ).astype(BF16)
                if rl == 0:
                    table[(20 + cl) * LEV : (21 + cl) * LEV, lanes] = pltpu.roll(x, 96, 1).astype(BF16)


def corner_lines(obs, turn, f):
    turn[...] = jnp.zeros_like(turn)
    row = OBS + f
    half = lax.broadcasted_iota(jnp.int32, (1, CY), 1) < CY // 2
    for move_y, c in ((1, 0), (-1, CY - 2)):
        upper = obs[diagonal(-1, move_y), row : row + 1, :]
        lower = obs[diagonal(1, move_y), row : row + 1, :]
        turn[c : c + 1, :] = jnp.where(half, upper, pltpu.roll(lower, CY // 2, 1))
        turn[c + 1 : c + 2, :] = jnp.where(half, pltpu.roll(upper, CY // 2, 1), lower)
    spots = turn[...].T
    lane = lax.broadcasted_iota(jnp.int32, (LEV, CY), 1)
    none = jnp.zeros((LEV, CY), F32)
    lines = []
    for i in range(4):
        h = spots[i * LEV : (i + 1) * LEV, :]
        lines.append((none,) + tuple(shifted(lane, none, h, b) for b in (1, 2, -1, -2)))
    return lines


def corners(obs, u_in, v_in, t_in, hyper, damp, u_out, v_out, t_out, turn, coef, quarter):
    per_level(coef, quarter, hyper, damp)
    u_out[...] = u_in[...]
    v_out[...] = v_in[...]
    t_out[...] = t_in[...]
    lines = [corner_lines(obs, turn, f) for f in range(FIELDS)]
    none = jnp.zeros((LEV, CY), F32)
    for sign, near, far in ((-1, 1, 0), (1, 2, 3)):
        add_rows(
            u_out,
            v_out,
            t_out,
            [line[near] for line in lines],
            [line[far] for line in lines],
            sign,
            coef[...],
            quarter[...],
            none,
        )


def interpolate(start, obs, t, hyper, model, table, block, row, col, lev, turn, coef):
    table[...] = start[...]
    for k in range(LEV):
        coef[k : k + 1, :] = jnp.full((1, CY), hyper[k], F32)
    far_up, near_up, near_down, far_down = corner_lines(obs, turn, 2)
    terms = (
        one(near_up, -1) + two(far_up, -1),
        two(near_up, -1),
        two(near_down, 1),
        one(near_down, 1) + two(far_down, 1),
    )
    lane = lax.broadcasted_iota(jnp.int32, (LEV, CY), 1)
    for r, term in zip(ROWS, terms):
        value = t[pl.ds(r, LEV, stride=CX), :] - coef[...] * term
        for c in (0, 1, CY - 2, CY - 1):
            to = (r >> 2) * 32 + (c >> 2)
            moved = pltpu.roll(value, (to - c) % CY, 1)
            high = moved.astype(BF16).astype(F32)
            at = ((r & 3) * 5 + (c & 3)) * LEV
            for k, part in enumerate((high, moved - high)):
                old = table[at : at + LEV, k * CY : (k + 1) * CY].astype(F32)
                table[at : at + LEV, k * CY : (k + 1) * CY] = jnp.where(lane == to, part, old).astype(BF16)
    owners = model.shape[0]
    cell = obs[:, 0, :].astype(jnp.int32)
    c, r = cell & (CY - 1), cell >> 7
    block[...] = (r >> 2) * 32 + (c >> 2)
    row[...] = r & 3
    col[...] = c & 3
    lev[...] = obs[:, 1, :].astype(jnp.int32)
    wide = 256
    block_iota = lax.broadcasted_iota(jnp.int32, (128, wide), 0)
    lev_iota = lax.broadcasted_iota(jnp.int32, (LEV, wide), 0)

    def pair(p, carry):
        def two(ref):
            return jnp.concatenate([ref[pl.ds(2 * p, 1), :], ref[pl.ds(2 * p + 1, 1), :]], axis=1)

        def sent(k):
            return jnp.concatenate([obs[2 * p, k : k + 1, :], obs[2 * p + 1, k : k + 1, :]], axis=1)

        def bit(value, mask):
            return jnp.broadcast_to(value & mask, (LEV, wide)) != 0

        at, r, c, l = two(block), two(row), two(col), two(lev)
        a, w0, w1 = sent(2), sent(3), sent(4)
        w2 = 1.0 - w0 - w1
        hot = jnp.where(block_iota == at, 1.0, 0.0).astype(BF16)
        got = jnp.dot(
            table[...], jnp.concatenate([hot, hot], axis=0), preferred_element_type=F32
        )
        c1, c2, r1, r2 = bit(c, 1), bit(c, 2), bit(r, 1), bit(r, 2)
        here, beside = [], []
        for i in range(5):
            g = [got[(i * 5 + j) * LEV : (i * 5 + j + 1) * LEV, :] for j in range(5 if i < 4 else 4)]
            h1 = jnp.where(c2, g[3], g[1])
            here.append(jnp.where(c1, h1, jnp.where(c2, g[2], g[0])))
            if i < 4:
                beside.append(jnp.where(c1, jnp.where(c2, g[4], g[2]), h1))
        h0, h1, h2 = (jnp.where(r2, here[i + 2], here[i]) for i in range(3))
        t0, t1 = jnp.where(r1, h1, h0), jnp.where(r1, h2, h1)
        t2 = jnp.where(
            r1, jnp.where(r2, beside[3], beside[1]), jnp.where(r2, beside[2], beside[0])
        )
        weight = jnp.where(lev_iota == l, 1.0 - a, jnp.where(lev_iota == l + 1, a, 0.0))
        out = jnp.sum(weight * (w0 * t0 + w1 * t1 + w2 * t2), axis=0, keepdims=True)
        model[pl.ds(2 * p, 1), :] = out[:, :128]
        model[pl.ds(2 * p + 1, 1), :] = out[:, 128:]
        return carry

    lax.fori_loop(0, owners // 2, pair, 0, unroll=UNROLL)


def swap(axis, first):
    count = lax.axis_size(axis)
    pairs = [((i + first) % count, (i + first + 1) % count) for i in range(0, count, 2)]
    return pairs + [(b, a) for a, b in pairs]


def on_device(theta, wind_u, wind_v, hyper, damp, cells, levels, bary, vfrac, values, mask):
    u, v, t = (f.reshape(FLAT, CY) for f in (wind_u, wind_v, theta))
    owners, slots = cells.shape[1], cells.shape[2]
    shape = jax.ShapeDtypeStruct
    sent = pl.pallas_call(
        messages_out,
        out_shape=shape((owners, SENT, slots), F32),
        in_specs=[HBM] * 7,
        out_specs=HBM,
        scratch_shapes=[
            pltpu.VMEM((FIELDS, FLAT, CY), F32),
            pltpu.VMEM((2, owners, slots), jnp.int32),
            pltpu.VMEM((owners, slots), F32),
            pltpu.VMEM((2, owners, slots), F32),
            pltpu.VMEM((owners, SENT, slots), F32),
            pltpu.VMEM((CY, CY), F32),
            pltpu.SemaphoreType.DMA((7,)),
        ],
        compiler_params=WHOLE,
        cost_estimate=cost(100000, 3000000),
    )(u, v, t, cells[0], levels[0], jnp.swapaxes(bary[0], 0, 1), vfrac[0])
    got = lax.all_to_all(sent, BOTH, split_axis=0, concat_axis=0, tiled=True)
    columns = shape((2 * BLOCKS, CY), F32)
    edge = shape((EDGE, CY), F32)
    col_a, col_b, row_a, row_b = pl.pallas_call(
        edges_out,
        out_shape=(columns, columns, edge, edge),
        in_specs=[VMEM] * 3,
        compiler_params=PARAMS,
        cost_estimate=cost(100000, 1000000),
    )(u, v, t)
    col_b = lax.ppermute(col_b, "py", swap("py", 1))
    col_a = lax.ppermute(col_a, "py", swap("py", 0))
    row_b = lax.ppermute(row_b, "px", swap("px", 1))
    row_a = lax.ppermute(row_a, "px", swap("px", 0))
    pick = pl.pallas_call(
        selector,
        out_shape=shape((4 * CY, 4 * CY), BF16),
        compiler_params=PARAMS,
        cost_estimate=cost(1000000, 500000),
    )()
    patch = shape((FLAT, CY), F32)
    turn = pltpu.VMEM((CY, CY), F32)
    each = pltpu.VMEM((LEV, CY), F32)
    u_most, v_most, t_most, table = pl.pallas_call(
        step,
        out_shape=(patch, patch, patch, shape((24 * LEV, 2 * CY), BF16)),
        in_specs=[VMEM] * 7 + [SMEM] * 2 + [VMEM],
        scratch_shapes=[pltpu.VMEM((FIELDS * FLAT, CY), F32), turn, each, each],
        compiler_params=PARAMS,
        cost_estimate=cost(8000000, 3000000),
    )(u, v, t, col_a, col_b, row_a, row_b, hyper, damp, pick)
    model = pl.pallas_call(
        interpolate,
        out_shape=shape((owners, slots), F32),
        in_specs=[VMEM] * 3 + [SMEM],
        scratch_shapes=[pltpu.VMEM((24 * LEV, 2 * CY), BF16)]
        + [pltpu.VMEM((owners, slots), jnp.int32)] * 4
        + [turn, each],
        compiler_params=PARAMS,
        cost_estimate=cost(6500000000, 1000000),
    )(table, got, t_most, hyper)
    u_next, v_next, t_next = pl.pallas_call(
        corners,
        out_shape=(patch, patch, patch),
        in_specs=[VMEM] * 4 + [SMEM] * 2,
        scratch_shapes=[turn, each, each],
        compiler_params=PARAMS,
        cost_estimate=cost(4000000, 3000000),
    )(got, u_most, v_most, t_most, hyper, damp)
    back = lax.all_to_all(model, BOTH, split_axis=0, concat_axis=0, tiled=True)
    departures = mask.astype(F32) * (values - back[None])
    whole = theta.shape
    return t_next.reshape(whole), u_next.reshape(whole), v_next.reshape(whole), departures


def solution(mesh):
    field = P(None, "px", "py")
    obs = P(BOTH, None, None)
    return jax.shard_map(
        on_device,
        mesh=mesh,
        in_specs=(field, field, field, P(), P(), obs, obs, P(BOTH, None, None, None), obs, obs, obs),
        out_specs=(field, field, field, obs),
        check_vma=False,
    )
```

```python
import jax
import jax.numpy as jnp
from jax import lax
from jax.experimental import pallas as pl
from jax.experimental.pallas import tpu as pltpu
from jax.sharding import PartitionSpec as P

LEV = 32
CX = 16
CY = 128
FLAT = LEV * CX
FIELDS = 3
OBS = 5
SENT = OBS + FIELDS
ROWS = (0, 1, CX - 2, CX - 1)
BLOCKS = FIELDS * FLAT // 128
EDGE = 2 * FIELDS * LEV
UNROLL = 32
BOTH = ("px", "py")
F32 = jnp.float32
BF16 = jnp.bfloat16
VMEM = pl.BlockSpec(memory_space=pltpu.VMEM)
SMEM = pl.BlockSpec(memory_space=pltpu.SMEM)
HBM = pl.BlockSpec(memory_space=pltpu.MemorySpace.HBM)
PARAMS = pltpu.CompilerParams(vmem_limit_bytes=48 << 20)


WHOLE = pltpu.CompilerParams(vmem_limit_bytes=60 << 20)


def cost(flops, moved):
    return pl.CostEstimate(flops=flops, bytes_accessed=moved, transcendentals=0)


def diagonal(move_x, move_y):
    count_x, count_y = lax.axis_size("px"), lax.axis_size("py")
    x = lax.rem(lax.axis_index("px") + count_x + move_x, count_x)
    return x * count_y + lax.rem(lax.axis_index("py") + count_y + move_y, count_y)


def messages_out(u, v, t, cells, levels, bary, vfrac, sent, fields, ints, floats, weights, packed, turn, sems):
    copies = [
        pltpu.make_async_copy(u, fields.at[0], sems.at[0]),
        pltpu.make_async_copy(v, fields.at[1], sems.at[1]),
        pltpu.make_async_copy(t, fields.at[2], sems.at[2]),
        pltpu.make_async_copy(cells, ints.at[0], sems.at[3]),
        pltpu.make_async_copy(levels, ints.at[1], sems.at[4]),
        pltpu.make_async_copy(vfrac, floats, sems.at[5]),
        pltpu.make_async_copy(bary.at[pl.ds(0, 2)], weights, sems.at[6]),
    ]
    for copy in copies:
        copy.start()
    packed[:, OBS:, :] = jnp.zeros((packed.shape[0], FIELDS, CY), F32)
    for copy in copies:
        copy.wait()
    packed[:, 0, :] = ints[0].astype(F32)
    packed[:, 1, :] = ints[1].astype(F32)
    packed[:, 2, :] = floats[...]
    packed[:, 3, :] = weights[0]
    packed[:, 4, :] = weights[1]
    half = lax.broadcasted_iota(jnp.int32, (1, CY), 1) < CY // 2
    for f in range(FIELDS):
        for i, r in enumerate(ROWS):
            turn[i * LEV : (i + 1) * LEV, :] = fields[f, pl.ds(r, LEV, stride=CX), :]
        turned = turn[...].T
        for move_y, c in ((-1, 0), (1, CY - 2)):
            one, two = turned[c : c + 1, :], turned[c + 1 : c + 2, :]
            row = OBS + f
            packed[diagonal(-1, move_y), row : row + 1, :] = jnp.where(
                half, one, pltpu.roll(two, CY // 2, 1)
            )
            packed[diagonal(1, move_y), row : row + 1, :] = jnp.where(
                half, pltpu.roll(one, CY // 2, 1), two
            )
    pltpu.sync_copy(packed, sent)


def is_even(axis):
    return lax.rem(lax.axis_index(axis), 2) == 0


def edges_out(u, v, t, col_a, col_b, row_a, row_b):
    even_x, even_y = is_even("px"), is_even("py")
    for f, field in enumerate((u, v, t)):
        for i in range(2):
            at = (i * FIELDS + f) * LEV
            low = field[pl.ds(i, LEV, stride=CX), :]
            high = field[pl.ds(CX - 2 + i, LEV, stride=CX), :]
            row_a[at : at + LEV, :] = jnp.where(even_x, high, low)
            row_b[at : at + LEV, :] = jnp.where(even_x, low, high)
        for k in range(FLAT // 128):
            turned = field[k * 128 : (k + 1) * 128, :].T
            first, last = turned[0:2, :], turned[CY - 2 :, :]
            at = 2 * (f * FLAT // 128 + k)
            col_a[at : at + 2, :] = jnp.where(even_y, last, first)
            col_b[at : at + 2, :] = jnp.where(even_y, first, last)


def shifted(lane, field, border, b):
    if b > 0:
        return pltpu.roll(jnp.where(lane < b, border, field), CY - b, 1)
    return pltpu.roll(jnp.where(lane >= CY + b, border, field), -b, 1)


def per_level(coef, quarter, hyper, damp):
    for lev in range(LEV):
        coef[lev : lev + 1, :] = jnp.full((1, CY), hyper[lev], F32)
        quarter[lev : lev + 1, :] = jnp.full((1, CY), damp[lev] * 0.25, F32)


def one(line, sign):
    c, e1, e2, w1, w2 = line
    if sign > 0:
        return 2.0 * (e1 + w2) - 10.0 * (c + w1)
    return 2.0 * (w1 + e2) - 10.0 * (c + e1)


def two(line, sign):
    c, e1, e2, w1, w2 = line
    return c + w2 + 2.0 * w1 if sign > 0 else c + e2 + 2.0 * e1


def add(out, r, value):
    out[pl.ds(r, LEV, stride=CX), :] += value


def add_rows(u_out, v_out, t_out, near, far, sign, k4, k2, wind):
    edge, following = (CX - 1, CX - 2) if sign > 0 else (0, 1)
    cross = [line[1] - line[3] for line in near]
    fourth = [one(near[f], sign) + two(far[f], sign) for f in range(FIELDS)]
    add(u_out, edge, k2 * (far[0][0] + sign * cross[1]) - k4 * fourth[0])
    add(u_out, following, k2 * near[0][0] - k4 * two(near[0], sign))
    add(v_out, edge, k2 * (sign * cross[0]) - k4 * fourth[1])
    add(v_out, following, -k4 * two(near[1], sign))
    add(t_out, edge, -k4 * fourth[2] - (0.25 * sign) * wind * near[2][0])
    add(t_out, following, -k4 * two(near[2], sign))


def bulk(u, v, t, hyper, damp, u_out, v_out, t_out, pick):
    lane = lax.broadcasted_iota(jnp.int32, (CX, CY), 1)
    none = jnp.zeros((8, CY), F32)

    def rows(value, a):
        return pltpu.roll(jnp.concatenate([value, none], axis=0), -a % (CX + 8), 0)[:CX, :]

    def level(lev, carry):
        coef = hyper[lev]
        quarter = damp[lev] * 0.25
        at = pl.multiple_of(lev * CX, 8)
        views = []
        fourth = []
        for field in (u, v, t):
            c = field[pl.ds(at, CX), :]
            e1, e2, w1, w2 = (shifted(lane, c, 0.0, b) for b in (1, 2, -1, -2))
            total = 42.0 * c - 10.0 * (e1 + w1) + (e2 + w2)
            total = total + rows(2.0 * (e1 + w2) - 10.0 * (c + w1), 1)
            total = total + rows(2.0 * (w1 + e2) - 10.0 * (c + e1), -1)
            total = total + rows(c + w2 + 2.0 * w1, 2) + rows(c + e2 + 2.0 * e1, -2)
            fourth.append(total)
            views.append((c, e1, w1, e2, w2))
        (u0, ue, uw, _, _), (v0, ve, vw, ve2, vw2), (t0, te, tw, _, _) = views
        du, dv = ue - uw, ve - vw
        uxx = rows(u0, 2) - 2.0 * u0 + rows(u0, -2)
        vxy = rows(dv, 1) - rows(dv, -1)
        uxy = rows(du, 1) - rows(du, -1)
        vyy = ve2 - 2.0 * v0 + vw2
        u_out[pl.ds(at, CX), :] = u0 - coef * fourth[0] + quarter * (uxx + vxy)
        v_out[pl.ds(at, CX), :] = v0 - coef * fourth[1] + quarter * (uxy + vyy)
        drift = u0 * (rows(t0, 1) - rows(t0, -1)) + v0 * (te - tw)
        t_out[pl.ds(at, CX), :] = t0 - coef * fourth[2] - 0.25 * drift
        return carry

    lax.fori_loop(0, LEV, level, 0, unroll=4)
    k = lax.broadcasted_iota(jnp.int32, pick.shape, 0)
    n = lax.broadcasted_iota(jnp.int32, pick.shape, 1)
    want = ((n >> 5) & 3) * CY + (n & 31) * 4 + (n >> 7)
    pick[...] = jnp.where(k == want, 1.0, 0.0).astype(BF16)


def borders(
    u, u_in, v_in, t_in, own_a, own_b, col_a, col_b, row_a, row_b, hyper, damp, pick,
    u_out, v_out, t_out, table, coef, quarter, turn, across,
):
    even_x, even_y = is_even("px"), is_even("py")
    per_level(coef, quarter, hyper, damp)
    parts = FLAT // 128
    spot = lax.broadcasted_iota(jnp.int32, (1, CY), 1) >> 4
    for k in range(parts):
        c, q = jnp.zeros((1, CY), F32), jnp.zeros((1, CY), F32)
        for i in range(8):
            c = jnp.where(spot == i, hyper[8 * k + i], c)
            q = jnp.where(spot == i, damp[8 * k + i] * 0.25, q)
        across[k : k + 1, :] = c
        across[parts + k : parts + k + 1, :] = q
    c4, q4 = across[0:parts, :], across[parts : 2 * parts, :]
    place = lax.broadcasted_iota(jnp.int32, (parts, CY), 1) & (CX - 1)

    def moved(x, a):
        inside = place < CX - a if a > 0 else place >= -a
        return jnp.where(inside, pltpu.roll(x, -a % CY, 1), 0.0)

    def line(yes, no, f, col):
        at = pl.ds(2 * parts * f + col, parts, stride=2)
        return jnp.where(even_y, yes[at, :], no[at, :])

    east = [[line(col_a, col_b, f, i) for i in range(2)] for f in range(FIELDS)]
    west = [[line(col_b, col_a, f, i) for i in (1, 0)] for f in range(FIELDS)]
    v_first, v_last = line(own_b, own_a, 1, 0), line(own_a, own_b, 1, 1)

    def nearest(x, y, s):
        total = 2.0 * moved(x, s) - 10.0 * (x + moved(x, -s)) + 2.0 * moved(x, -2 * s)
        return total + next_one(y, s)

    def next_one(x, s):
        return x + 2.0 * moved(x, -s) + moved(x, -2 * s)

    def slope(x):
        return moved(x, 1) - moved(x, -1)

    (ue, ve, te), (uw, vw, tw) = east, west
    terms = (
        (
            -c4 * nearest(*uw, -1) - q4 * slope(vw[0]),
            -c4 * next_one(uw[0], -1),
            -c4 * next_one(ue[0], 1),
            -c4 * nearest(*ue, 1) + q4 * slope(ve[0]),
        ),
        (
            -c4 * nearest(*vw, -1) + q4 * (vw[1] - slope(uw[0])),
            -c4 * next_one(vw[0], -1) + q4 * vw[0],
            -c4 * next_one(ve[0], 1) + q4 * ve[0],
            -c4 * nearest(*ve, 1) + q4 * (ve[1] + slope(ue[0])),
        ),
        (
            -c4 * nearest(*tw, -1) + 0.25 * v_first * tw[0],
            -c4 * next_one(tw[0], -1),
            -c4 * next_one(te[0], 1),
            -c4 * nearest(*te, 1) - 0.25 * v_last * te[0],
        ),
    )
    turn[...] = jnp.zeros_like(turn)
    for f, (start, out) in enumerate(((u_in, u_out), (v_in, v_out), (t_in, t_out))):
        for k in range(parts):
            for col, term in zip((0, 1, CY - 2, CY - 1), terms[f]):
                turn[col : col + 1, :] = term[k : k + 1, :]
            out[k * 128 : (k + 1) * 128, :] = start[k * 128 : (k + 1) * 128, :] + turn[...].T
    lane = lax.broadcasted_iota(jnp.int32, (LEV, CY), 1)

    def outside(this, other, keep, i):
        line = []
        for f in range(FIELDS):
            at = (i * FIELDS + f) * LEV
            c = jnp.where(keep, this[at : at + LEV, :], other[at : at + LEV, :])
            line.append((c,) + tuple(shifted(lane, c, 0.0, b) for b in (1, 2, -1, -2)))
        return line

    for sign, this, other, near, far in ((-1, row_b, row_a, 1, 0), (1, row_a, row_b, 0, 1)):
        wind = u[pl.ds(0 if sign < 0 else CX - 1, LEV, stride=CX), :]
        add_rows(
            u_out,
            v_out,
            t_out,
            outside(this, other, even_x, near),
            outside(this, other, even_x, far),
            sign,
            coef[...],
            quarter[...],
            wind,
        )
    for rl in range(4):
        parts = [t_out[pl.ds(4 * rh + rl, LEV, stride=CX), :] for rh in range(4)]
        tops = [part.astype(BF16) for part in parts]
        rests = [(part - top.astype(F32)).astype(BF16) for part, top in zip(parts, tops)]
        both = jnp.concatenate(
            [jnp.concatenate(tops, axis=1), jnp.concatenate(rests, axis=1)], axis=0
        )
        put = jnp.dot(both, pick[...], preferred_element_type=F32)
        for half in range(2):
            lanes = slice(half * 128, half * 128 + 128)
            for cl in range(4):
                x = put[half * LEV : (half + 1) * LEV, cl * 128 : (cl + 1) * 128]
                table[(rl * 5 + cl) * LEV : (rl * 5 + cl + 1) * LEV, lanes] = x.astype(BF16)
                if cl == 0:
                    table[(rl * 5 + 4) * LEV : (rl * 5 + 5) * LEV, lanes] = pltpu.roll(
                        x, 127, 1
                    ).astype(BF16)
                if rl == 0:
                    table[(20 + cl) * LEV : (21 + cl) * LEV, lanes] = pltpu.roll(x, 96, 1).astype(BF16)


def corner_lines(obs, turn, f):
    turn[...] = jnp.zeros_like(turn)
    row = OBS + f
    half = lax.broadcasted_iota(jnp.int32, (1, CY), 1) < CY // 2
    for move_y, c in ((1, 0), (-1, CY - 2)):
        upper = obs[diagonal(-1, move_y), row : row + 1, :]
        lower = obs[diagonal(1, move_y), row : row + 1, :]
        turn[c : c + 1, :] = jnp.where(half, upper, pltpu.roll(lower, CY // 2, 1))
        turn[c + 1 : c + 2, :] = jnp.where(half, pltpu.roll(upper, CY // 2, 1), lower)
    spots = turn[...].T
    lane = lax.broadcasted_iota(jnp.int32, (LEV, CY), 1)
    none = jnp.zeros((LEV, CY), F32)
    lines = []
    for i in range(4):
        h = spots[i * LEV : (i + 1) * LEV, :]
        lines.append((none,) + tuple(shifted(lane, none, h, b) for b in (1, 2, -1, -2)))
    return lines


def corners(obs, u_in, v_in, t_in, coef, quarter, u_out, v_out, t_out, turn):
    u_out[...] = u_in[...]
    v_out[...] = v_in[...]
    t_out[...] = t_in[...]
    lines = [corner_lines(obs, turn, f) for f in range(FIELDS)]
    none = jnp.zeros((LEV, CY), F32)
    for sign, near, far in ((-1, 1, 0), (1, 2, 3)):
        add_rows(
            u_out,
            v_out,
            t_out,
            [line[near] for line in lines],
            [line[far] for line in lines],
            sign,
            coef[...],
            quarter[...],
            none,
        )


def interpolate(start, obs, t, coef, table, model, block, row, col, lev, turn):
    far_up, near_up, near_down, far_down = corner_lines(obs, turn, 2)
    terms = (
        one(near_up, -1) + two(far_up, -1),
        two(near_up, -1),
        two(near_down, 1),
        one(near_down, 1) + two(far_down, 1),
    )
    lane = lax.broadcasted_iota(jnp.int32, (LEV, CY), 1)
    for r, term in zip(ROWS, terms):
        value = t[pl.ds(r, LEV, stride=CX), :] - coef[...] * term
        for c in (0, 1, CY - 2, CY - 1):
            to = (r >> 2) * 32 + (c >> 2)
            moved = pltpu.roll(value, (to - c) % CY, 1)
            high = moved.astype(BF16).astype(F32)
            at = ((r & 3) * 5 + (c & 3)) * LEV
            for k, part in enumerate((high, moved - high)):
                old = start[at : at + LEV, k * CY : (k + 1) * CY].astype(F32)
                table[at : at + LEV, k * CY : (k + 1) * CY] = jnp.where(lane == to, part, old).astype(BF16)
    owners = model.shape[0]
    cell = obs[:, 0, :].astype(jnp.int32)
    c, r = cell & (CY - 1), cell >> 7
    block[...] = (r >> 2) * 32 + (c >> 2)
    row[...] = r & 3
    col[...] = c & 3
    lev[...] = obs[:, 1, :].astype(jnp.int32)
    wide = 256
    block_iota = lax.broadcasted_iota(jnp.int32, (128, wide), 0)
    lev_iota = lax.broadcasted_iota(jnp.int32, (LEV, wide), 0)

    def pair(p, carry):
        def two(ref):
            return jnp.concatenate([ref[pl.ds(2 * p, 1), :], ref[pl.ds(2 * p + 1, 1), :]], axis=1)

        def sent(k):
            return jnp.concatenate([obs[2 * p, k : k + 1, :], obs[2 * p + 1, k : k + 1, :]], axis=1)

        def bit(value, mask):
            return jnp.broadcast_to(value & mask, (LEV, wide)) != 0

        at, r, c, l = two(block), two(row), two(col), two(lev)
        a, w0, w1 = sent(2), sent(3), sent(4)
        w2 = 1.0 - w0 - w1
        hot = jnp.where(block_iota == at, 1.0, 0.0).astype(BF16)
        got = jnp.dot(
            table[...], jnp.concatenate([hot, hot], axis=0), preferred_element_type=F32
        )
        c1, c2, r1, r2 = bit(c, 1), bit(c, 2), bit(r, 1), bit(r, 2)
        here, beside = [], []
        for i in range(5):
            g = [got[(i * 5 + j) * LEV : (i * 5 + j + 1) * LEV, :] for j in range(5 if i < 4 else 4)]
            h1 = jnp.where(c2, g[3], g[1])
            here.append(jnp.where(c1, h1, jnp.where(c2, g[2], g[0])))
            if i < 4:
                beside.append(jnp.where(c1, jnp.where(c2, g[4], g[2]), h1))
        h0, h1, h2 = (jnp.where(r2, here[i + 2], here[i]) for i in range(3))
        t0, t1 = jnp.where(r1, h1, h0), jnp.where(r1, h2, h1)
        t2 = jnp.where(
            r1, jnp.where(r2, beside[3], beside[1]), jnp.where(r2, beside[2], beside[0])
        )
        weight = jnp.where(lev_iota == l, 1.0 - a, jnp.where(lev_iota == l + 1, a, 0.0))
        out = jnp.sum(weight * (w0 * t0 + w1 * t1 + w2 * t2), axis=0, keepdims=True)
        model[pl.ds(2 * p, 1), :] = out[:, :128]
        model[pl.ds(2 * p + 1, 1), :] = out[:, 128:]
        return carry

    lax.fori_loop(0, owners // 2, pair, 0, unroll=UNROLL)


def swap(axis, first):
    count = lax.axis_size(axis)
    pairs = [((i + first) % count, (i + first + 1) % count) for i in range(0, count, 2)]
    return pairs + [(b, a) for a, b in pairs]


def on_device(theta, wind_u, wind_v, hyper, damp, cells, levels, bary, vfrac, values, mask):
    u, v, t = (f.reshape(FLAT, CY) for f in (wind_u, wind_v, theta))
    owners, slots = cells.shape[1], cells.shape[2]
    shape = jax.ShapeDtypeStruct
    sent = pl.pallas_call(
        messages_out,
        out_shape=shape((owners, SENT, slots), F32),
        in_specs=[HBM] * 7,
        out_specs=HBM,
        scratch_shapes=[
            pltpu.VMEM((FIELDS, FLAT, CY), F32),
            pltpu.VMEM((2, owners, slots), jnp.int32),
            pltpu.VMEM((owners, slots), F32),
            pltpu.VMEM((2, owners, slots), F32),
            pltpu.VMEM((owners, SENT, slots), F32),
            pltpu.VMEM((CY, CY), F32),
            pltpu.SemaphoreType.DMA((7,)),
        ],
        compiler_params=WHOLE,
        cost_estimate=cost(100000, 3000000),
    )(u, v, t, cells[0], levels[0], jnp.swapaxes(bary[0], 0, 1), vfrac[0])
    got = lax.all_to_all(sent, BOTH, split_axis=0, concat_axis=0, tiled=True)
    columns = shape((2 * BLOCKS, CY), F32)
    edge = shape((EDGE, CY), F32)
    own_a, own_b, row_a, row_b = pl.pallas_call(
        edges_out,
        out_shape=(columns, columns, edge, edge),
        in_specs=[VMEM] * 3,
        compiler_params=PARAMS,
        cost_estimate=cost(100000, 1000000),
    )(u, v, t)
    col_b = lax.ppermute(own_b, "py", swap("py", 1))
    col_a = lax.ppermute(own_a, "py", swap("py", 0))
    row_b = lax.ppermute(row_b, "px", swap("px", 1))
    row_a = lax.ppermute(row_a, "px", swap("px", 0))
    patch = shape((FLAT, CY), F32)
    plane = shape((LEV, CY), F32)
    grid = shape((24 * LEV, 2 * CY), BF16)
    turn = pltpu.VMEM((CY, CY), F32)
    u_part, v_part, t_part, pick = pl.pallas_call(
        bulk,
        out_shape=(patch, patch, patch, shape((4 * CY, 4 * CY), BF16)),
        in_specs=[VMEM] * 3 + [SMEM] * 2,
        compiler_params=PARAMS,
        cost_estimate=cost(8000000, 10000000),
    )(u, v, t, hyper, damp)
    u_most, v_most, t_most, table, coef, quarter = pl.pallas_call(
        borders,
        out_shape=(patch, patch, patch, grid, plane, plane),
        in_specs=[VMEM] * 10 + [SMEM] * 2 + [VMEM],
        scratch_shapes=[turn, pltpu.VMEM((8, CY), F32)],
        compiler_params=PARAMS,
        cost_estimate=cost(4000000, 3000000),
    )(u, u_part, v_part, t_part, own_a, own_b, col_a, col_b, row_a, row_b, hyper, damp, pick)
    _, model = pl.pallas_call(
        interpolate,
        out_shape=(grid, shape((owners, slots), F32)),
        in_specs=[VMEM] * 4,
        scratch_shapes=[pltpu.VMEM((owners, slots), jnp.int32)] * 4 + [turn],
        input_output_aliases={0: 0},
        compiler_params=PARAMS,
        cost_estimate=cost(6500000000, 1000000),
    )(table, got, t_most, coef)
    u_next, v_next, t_next = pl.pallas_call(
        corners,
        out_shape=(patch, patch, patch),
        in_specs=[VMEM] * 6,
        scratch_shapes=[turn],
        compiler_params=PARAMS,
        cost_estimate=cost(4000000, 3000000),
    )(got, u_most, v_most, t_most, coef, quarter)
    back = lax.all_to_all(model, BOTH, split_axis=0, concat_axis=0, tiled=True)
    departures = mask.astype(F32) * (values - back[None])
    whole = theta.shape
    return t_next.reshape(whole), u_next.reshape(whole), v_next.reshape(whole), departures


def solution(mesh):
    field = P(None, "px", "py")
    obs = P(BOTH, None, None)
    return jax.shard_map(
        on_device,
        mesh=mesh,
        in_specs=(field, field, field, P(), P(), obs, obs, P(BOTH, None, None, None), obs, obs, obs),
        out_specs=(field, field, field, obs),
        check_vma=False,
    )
```

```python
import jax
import jax.numpy as jnp
from jax import lax
from jax.experimental import pallas as pl
from jax.experimental.pallas import tpu as pltpu
from jax.sharding import PartitionSpec as P

LEV = 32
CX = 16
CY = 128
FLAT = LEV * CX
FIELDS = 3
OBS = 5
SENT = OBS + FIELDS
ROWS = (0, 1, CX - 2, CX - 1)
BLOCKS = FIELDS * FLAT // 128
EDGE = 2 * FIELDS * LEV
UNROLL = 32
BOTH = ("px", "py")
F32 = jnp.float32
BF16 = jnp.bfloat16
VMEM = pl.BlockSpec(memory_space=pltpu.VMEM)
SMEM = pl.BlockSpec(memory_space=pltpu.SMEM)
HBM = pl.BlockSpec(memory_space=pltpu.MemorySpace.HBM)
PARAMS = pltpu.CompilerParams(vmem_limit_bytes=48 << 20)


WHOLE = pltpu.CompilerParams(vmem_limit_bytes=60 << 20)


def cost(flops, moved):
    return pl.CostEstimate(flops=flops, bytes_accessed=moved, transcendentals=0)


def diagonal(move_x, move_y):
    count_x, count_y = lax.axis_size("px"), lax.axis_size("py")
    x = lax.rem(lax.axis_index("px") + count_x + move_x, count_x)
    return x * count_y + lax.rem(lax.axis_index("py") + count_y + move_y, count_y)


def messages_out(u, v, t, cells, levels, bary, vfrac, sent, fields, ints, floats, weights, packed, turn, sems):
    copies = [
        pltpu.make_async_copy(u, fields.at[0], sems.at[0]),
        pltpu.make_async_copy(v, fields.at[1], sems.at[1]),
        pltpu.make_async_copy(t, fields.at[2], sems.at[2]),
        pltpu.make_async_copy(cells, ints.at[0], sems.at[3]),
        pltpu.make_async_copy(levels, ints.at[1], sems.at[4]),
        pltpu.make_async_copy(vfrac, floats, sems.at[5]),
        pltpu.make_async_copy(bary.at[pl.ds(0, 2)], weights, sems.at[6]),
    ]
    for copy in copies:
        copy.start()
    packed[:, OBS:, :] = jnp.zeros((packed.shape[0], FIELDS, CY), F32)
    for copy in copies:
        copy.wait()
    packed[:, 0, :] = ints[0].astype(F32)
    packed[:, 1, :] = ints[1].astype(F32)
    packed[:, 2, :] = floats[...]
    packed[:, 3, :] = weights[0]
    packed[:, 4, :] = weights[1]
    half = lax.broadcasted_iota(jnp.int32, (1, CY), 1) < CY // 2
    for f in range(FIELDS):
        for i, r in enumerate(ROWS):
            turn[i * LEV : (i + 1) * LEV, :] = fields[f, pl.ds(r, LEV, stride=CX), :]
        turned = turn[...].T
        for move_y, c in ((-1, 0), (1, CY - 2)):
            one, two = turned[c : c + 1, :], turned[c + 1 : c + 2, :]
            row = OBS + f
            packed[diagonal(-1, move_y), row : row + 1, :] = jnp.where(
                half, one, pltpu.roll(two, CY // 2, 1)
            )
            packed[diagonal(1, move_y), row : row + 1, :] = jnp.where(
                half, pltpu.roll(one, CY // 2, 1), two
            )
    pltpu.sync_copy(packed, sent)


def is_even(axis):
    return lax.rem(lax.axis_index(axis), 2) == 0


def edges_out(u, v, t, col_a, col_b, row_a, row_b):
    even_x, even_y = is_even("px"), is_even("py")
    for f, field in enumerate((u, v, t)):
        for i in range(2):
            at = (i * FIELDS + f) * LEV
            low = field[pl.ds(i, LEV, stride=CX), :]
            high = field[pl.ds(CX - 2 + i, LEV, stride=CX), :]
            row_a[at : at + LEV, :] = jnp.where(even_x, high, low)
            row_b[at : at + LEV, :] = jnp.where(even_x, low, high)
        for k in range(FLAT // 128):
            turned = field[k * 128 : (k + 1) * 128, :].T
            first, last = turned[0:2, :], turned[CY - 2 :, :]
            at = 2 * (f * FLAT // 128 + k)
            col_a[at : at + 2, :] = jnp.where(even_y, last, first)
            col_b[at : at + 2, :] = jnp.where(even_y, first, last)


def shifted(lane, field, border, b):
    if b > 0:
        return pltpu.roll(jnp.where(lane < b, border, field), CY - b, 1)
    return pltpu.roll(jnp.where(lane >= CY + b, border, field), -b, 1)


def per_level(coef, quarter, hyper, damp):
    for lev in range(LEV):
        coef[lev : lev + 1, :] = jnp.full((1, CY), hyper[lev], F32)
        quarter[lev : lev + 1, :] = jnp.full((1, CY), damp[lev] * 0.25, F32)


def one(line, sign):
    c, e1, e2, w1, w2 = line
    if sign > 0:
        return 2.0 * (e1 + w2) - 10.0 * (c + w1)
    return 2.0 * (w1 + e2) - 10.0 * (c + e1)


def two(line, sign):
    c, e1, e2, w1, w2 = line
    return c + w2 + 2.0 * w1 if sign > 0 else c + e2 + 2.0 * e1


def add(out, r, value):
    out[pl.ds(r, LEV, stride=CX), :] += value


def border_rows(sign):
    return (CX - 1, CX - 2) if sign > 0 else (0, 1)


def add_theta_rows(t_out, near, far, sign, k4, wind):
    edge, following = border_rows(sign)
    add(t_out, edge, -k4 * (one(near, sign) + two(far, sign)) - (0.25 * sign) * wind * near[0])
    add(t_out, following, -k4 * two(near, sign))


def add_wind_rows(u_out, v_out, near, far, sign, k4, k2):
    edge, following = border_rows(sign)
    (u1, v1), (u2, v2) = near, far
    add(u_out, edge, k2 * (u2[0] + sign * (v1[1] - v1[3])) - k4 * (one(u1, sign) + two(u2, sign)))
    add(u_out, following, k2 * u1[0] - k4 * two(u1, sign))
    add(v_out, edge, k2 * (sign * (u1[1] - u1[3])) - k4 * (one(v1, sign) + two(v2, sign)))
    add(v_out, following, -k4 * two(v1, sign))


def bulk(u, v, t, hyper, damp, u_out, v_out, t_out, pick):
    lane = lax.broadcasted_iota(jnp.int32, (CX, CY), 1)
    none = jnp.zeros((8, CY), F32)

    def rows(value, a):
        return pltpu.roll(jnp.concatenate([value, none], axis=0), -a % (CX + 8), 0)[:CX, :]

    def level(lev, carry):
        coef = hyper[lev]
        quarter = damp[lev] * 0.25
        at = pl.multiple_of(lev * CX, 8)
        views = []
        fourth = []
        for field in (u, v, t):
            c = field[pl.ds(at, CX), :]
            e1, e2, w1, w2 = (shifted(lane, c, 0.0, b) for b in (1, 2, -1, -2))
            total = 42.0 * c - 10.0 * (e1 + w1) + (e2 + w2)
            total = total + rows(2.0 * (e1 + w2) - 10.0 * (c + w1), 1)
            total = total + rows(2.0 * (w1 + e2) - 10.0 * (c + e1), -1)
            total = total + rows(c + w2 + 2.0 * w1, 2) + rows(c + e2 + 2.0 * e1, -2)
            fourth.append(total)
            views.append((c, e1, w1, e2, w2))
        (u0, ue, uw, _, _), (v0, ve, vw, ve2, vw2), (t0, te, tw, _, _) = views
        du, dv = ue - uw, ve - vw
        uxx = rows(u0, 2) - 2.0 * u0 + rows(u0, -2)
        vxy = rows(dv, 1) - rows(dv, -1)
        uxy = rows(du, 1) - rows(du, -1)
        vyy = ve2 - 2.0 * v0 + vw2
        u_out[pl.ds(at, CX), :] = u0 - coef * fourth[0] + quarter * (uxx + vxy)
        v_out[pl.ds(at, CX), :] = v0 - coef * fourth[1] + quarter * (uxy + vyy)
        drift = u0 * (rows(t0, 1) - rows(t0, -1)) + v0 * (te - tw)
        t_out[pl.ds(at, CX), :] = t0 - coef * fourth[2] - 0.25 * drift
        return carry

    lax.fori_loop(0, LEV, level, 0, unroll=4)
    k = lax.broadcasted_iota(jnp.int32, pick.shape, 0)
    n = lax.broadcasted_iota(jnp.int32, pick.shape, 1)
    want = ((n >> 5) & 3) * CY + (n & 31) * 4 + (n >> 7)
    pick[...] = jnp.where(k == want, 1.0, 0.0).astype(BF16)


def level_rows(across, hyper, damp):
    parts = FLAT // 128
    spot = lax.broadcasted_iota(jnp.int32, (1, CY), 1) >> 4
    for k in range(parts):
        c, q = jnp.zeros((1, CY), F32), jnp.zeros((1, CY), F32)
        for i in range(8):
            c = jnp.where(spot == i, hyper[8 * k + i], c)
            q = jnp.where(spot == i, damp[8 * k + i] * 0.25, q)
        across[k : k + 1, :] = c
        across[parts + k : parts + k + 1, :] = q
    return across[0:parts, :], across[parts : 2 * parts, :]


def line(yes, no, keep, f, col):
    parts = FLAT // 128
    at = pl.ds(2 * parts * f + col, parts, stride=2)
    return jnp.where(keep, yes[at, :], no[at, :])


def beside(col_a, col_b, keep, f):
    east = [line(col_a, col_b, keep, f, i) for i in range(2)]
    west = [line(col_b, col_a, keep, f, i) for i in (1, 0)]
    return east, west


def moved(x, a):
    place = lax.broadcasted_iota(jnp.int32, x.shape, 1) & (CX - 1)
    inside = place < CX - a if a > 0 else place >= -a
    return jnp.where(inside, pltpu.roll(x, -a % CY, 1), 0.0)


def next_one(x, s):
    return x + 2.0 * moved(x, -s) + moved(x, -2 * s)


def nearest(x, y, s):
    total = 2.0 * moved(x, s) - 10.0 * (x + moved(x, -s)) + 2.0 * moved(x, -2 * s)
    return total + next_one(y, s)


def slope(x):
    return moved(x, 1) - moved(x, -1)


def add_columns(start, out, terms, turn):
    for k in range(FLAT // 128):
        for col, term in zip((0, 1, CY - 2, CY - 1), terms):
            turn[col : col + 1, :] = term[k : k + 1, :]
        out[k * 128 : (k + 1) * 128, :] = start[k * 128 : (k + 1) * 128, :] + turn[...].T


def outside(this, other, keep, f, i):
    lane = lax.broadcasted_iota(jnp.int32, (LEV, CY), 1)
    at = (i * FIELDS + f) * LEV
    c = jnp.where(keep, this[at : at + LEV, :], other[at : at + LEV, :])
    return (c,) + tuple(shifted(lane, c, 0.0, b) for b in (1, 2, -1, -2))


def theta_borders(
    u, t_in, own_a, own_b, col_b, col_a, row_a, row_b, hyper, damp, pick, t_out, table, coef, quarter, turn, across
):
    even_x, even_y = is_even("px"), is_even("py")
    per_level(coef, quarter, hyper, damp)
    c4, _ = level_rows(across, hyper, damp)
    east, west = beside(col_a, col_b, even_y, 2)
    v_first, v_last = line(own_b, own_a, even_y, 1, 0), line(own_a, own_b, even_y, 1, 1)
    turn[...] = jnp.zeros_like(turn)
    terms = (
        -c4 * nearest(*west, -1) + 0.25 * v_first * west[0],
        -c4 * next_one(west[0], -1),
        -c4 * next_one(east[0], 1),
        -c4 * nearest(*east, 1) - 0.25 * v_last * east[0],
    )
    add_columns(t_in, t_out, terms, turn)
    for sign, this, other, near, far in ((-1, row_b, row_a, 1, 0), (1, row_a, row_b, 0, 1)):
        wind = u[pl.ds(border_rows(sign)[0], LEV, stride=CX), :]
        near, far = (outside(this, other, even_x, 2, i) for i in (near, far))
        add_theta_rows(t_out, near, far, sign, coef[...], wind)
    both = []
    for rl in range(4):
        parts = [t_out[pl.ds(4 * rh + rl, LEV, stride=CX), :] for rh in range(4)]
        tops = [part.astype(BF16) for part in parts]
        rests = [(part - top.astype(F32)).astype(BF16) for part, top in zip(parts, tops)]
        both += [jnp.concatenate(tops, axis=1), jnp.concatenate(rests, axis=1)]
    put = jnp.dot(jnp.concatenate(both, axis=0), pick[...], preferred_element_type=F32)
    for rl in range(4):
        for half in range(2):
            lanes = slice(half * 128, half * 128 + 128)
            for cl in range(4):
                at = (2 * rl + half) * LEV
                x = put[at : at + LEV, cl * 128 : (cl + 1) * 128]
                table[(rl * 5 + cl) * LEV : (rl * 5 + cl + 1) * LEV, lanes] = x.astype(BF16)
                if cl == 0:
                    table[(rl * 5 + 4) * LEV : (rl * 5 + 5) * LEV, lanes] = pltpu.roll(
                        x, 127, 1
                    ).astype(BF16)
                if rl == 0:
                    table[(20 + cl) * LEV : (21 + cl) * LEV, lanes] = pltpu.roll(x, 96, 1).astype(BF16)


def corner_lines(obs, turn, f):
    turn[...] = jnp.zeros_like(turn)
    row = OBS + f
    half = lax.broadcasted_iota(jnp.int32, (1, CY), 1) < CY // 2
    for move_y, c in ((1, 0), (-1, CY - 2)):
        upper = obs[diagonal(-1, move_y), row : row + 1, :]
        lower = obs[diagonal(1, move_y), row : row + 1, :]
        turn[c : c + 1, :] = jnp.where(half, upper, pltpu.roll(lower, CY // 2, 1))
        turn[c + 1 : c + 2, :] = jnp.where(half, pltpu.roll(upper, CY // 2, 1), lower)
    spots = turn[...].T
    lane = lax.broadcasted_iota(jnp.int32, (LEV, CY), 1)
    none = jnp.zeros((LEV, CY), F32)
    lines = []
    for i in range(4):
        h = spots[i * LEV : (i + 1) * LEV, :]
        lines.append((none,) + tuple(shifted(lane, none, h, b) for b in (1, 2, -1, -2)))
    return lines


def rest(
    u_in, v_in, t_in, col_b, col_a, row_a, row_b, obs, coef, quarter, hyper, damp, u_out, v_out, t_out, turn, across
):
    even_x, even_y = is_even("px"), is_even("py")
    c4, q4 = level_rows(across, hyper, damp)
    ue, uw = beside(col_a, col_b, even_y, 0)
    ve, vw = beside(col_a, col_b, even_y, 1)
    turn[...] = jnp.zeros_like(turn)
    add_columns(
        u_in,
        u_out,
        (
            -c4 * nearest(*uw, -1) - q4 * slope(vw[0]),
            -c4 * next_one(uw[0], -1),
            -c4 * next_one(ue[0], 1),
            -c4 * nearest(*ue, 1) + q4 * slope(ve[0]),
        ),
        turn,
    )
    add_columns(
        v_in,
        v_out,
        (
            -c4 * nearest(*vw, -1) + q4 * (vw[1] - slope(uw[0])),
            -c4 * next_one(vw[0], -1) + q4 * vw[0],
            -c4 * next_one(ve[0], 1) + q4 * ve[0],
            -c4 * nearest(*ve, 1) + q4 * (ve[1] + slope(ue[0])),
        ),
        turn,
    )
    t_out[...] = t_in[...]
    lines = [corner_lines(obs, turn, f) for f in range(FIELDS)]
    none = jnp.zeros((LEV, CY), F32)
    for sign, this, other, near, far in ((-1, row_b, row_a, 1, 0), (1, row_a, row_b, 0, 1)):
        spot = 0 if sign < 0 else 2
        straight = [[outside(this, other, even_x, f, i) for f in range(2)] for i in (near, far)]
        corner = [[lines[f][spot + i] for f in range(FIELDS)] for i in (near, far)]
        both = [
            [tuple(p + q for p, q in zip(straight[i][f], corner[i][f])) for f in range(2)] for i in range(2)
        ]
        add_wind_rows(u_out, v_out, both[0], both[1], sign, coef[...], quarter[...])
        add_theta_rows(t_out, corner[0][2], corner[1][2], sign, coef[...], none)


def interpolate(start, obs, t, coef, table, model, block, row, col, lev, turn):
    far_up, near_up, near_down, far_down = corner_lines(obs, turn, 2)
    terms = (
        one(near_up, -1) + two(far_up, -1),
        two(near_up, -1),
        two(near_down, 1),
        one(near_down, 1) + two(far_down, 1),
    )
    lane = lax.broadcasted_iota(jnp.int32, (LEV, CY), 1)
    for r, term in zip(ROWS, terms):
        value = t[pl.ds(r, LEV, stride=CX), :] - coef[...] * term
        for c in (0, 1, CY - 2, CY - 1):
            to = (r >> 2) * 32 + (c >> 2)
            moved = pltpu.roll(value, (to - c) % CY, 1)
            high = moved.astype(BF16).astype(F32)
            at = ((r & 3) * 5 + (c & 3)) * LEV
            for k, part in enumerate((high, moved - high)):
                old = start[at : at + LEV, k * CY : (k + 1) * CY].astype(F32)
                table[at : at + LEV, k * CY : (k + 1) * CY] = jnp.where(lane == to, part, old).astype(BF16)
    owners = model.shape[0]
    cell = obs[:, 0, :].astype(jnp.int32)
    c, r = cell & (CY - 1), cell >> 7
    block[...] = (r >> 2) * 32 + (c >> 2)
    row[...] = r & 3
    col[...] = c & 3
    lev[...] = obs[:, 1, :].astype(jnp.int32)
    wide = 256
    block_iota = lax.broadcasted_iota(jnp.int32, (128, wide), 0)
    lev_iota = lax.broadcasted_iota(jnp.int32, (LEV, wide), 0)

    def pair(p, carry):
        def two(ref):
            return jnp.concatenate([ref[pl.ds(2 * p, 1), :], ref[pl.ds(2 * p + 1, 1), :]], axis=1)

        def sent(k):
            return jnp.concatenate([obs[2 * p, k : k + 1, :], obs[2 * p + 1, k : k + 1, :]], axis=1)

        def bit(value, mask):
            return jnp.broadcast_to(value & mask, (LEV, wide)) != 0

        at, r, c, l = two(block), two(row), two(col), two(lev)
        a, w0, w1 = sent(2), sent(3), sent(4)
        w2 = 1.0 - w0 - w1
        hot = jnp.where(block_iota == at, 1.0, 0.0).astype(BF16)
        got = jnp.dot(
            table[...], jnp.concatenate([hot, hot], axis=0), preferred_element_type=F32
        )
        c1, c2, r1, r2 = bit(c, 1), bit(c, 2), bit(r, 1), bit(r, 2)
        here, beside = [], []
        for i in range(5):
            g = [got[(i * 5 + j) * LEV : (i * 5 + j + 1) * LEV, :] for j in range(5 if i < 4 else 4)]
            h1 = jnp.where(c2, g[3], g[1])
            here.append(jnp.where(c1, h1, jnp.where(c2, g[2], g[0])))
            if i < 4:
                beside.append(jnp.where(c1, jnp.where(c2, g[4], g[2]), h1))
        h0, h1, h2 = (jnp.where(r2, here[i + 2], here[i]) for i in range(3))
        t0, t1 = jnp.where(r1, h1, h0), jnp.where(r1, h2, h1)
        t2 = jnp.where(
            r1, jnp.where(r2, beside[3], beside[1]), jnp.where(r2, beside[2], beside[0])
        )
        weight = jnp.where(lev_iota == l, 1.0 - a, jnp.where(lev_iota == l + 1, a, 0.0))
        out = jnp.sum(weight * (w0 * t0 + w1 * t1 + w2 * t2), axis=0, keepdims=True)
        model[pl.ds(2 * p, 1), :] = out[:, :128]
        model[pl.ds(2 * p + 1, 1), :] = out[:, 128:]
        return carry

    lax.fori_loop(0, owners // 2, pair, 0, unroll=UNROLL)


def swap(axis, first):
    count = lax.axis_size(axis)
    pairs = [((i + first) % count, (i + first + 1) % count) for i in range(0, count, 2)]
    return pairs + [(b, a) for a, b in pairs]


def on_device(theta, wind_u, wind_v, hyper, damp, cells, levels, bary, vfrac, values, mask):
    u, v, t = (f.reshape(FLAT, CY) for f in (wind_u, wind_v, theta))
    owners, slots = cells.shape[1], cells.shape[2]
    shape = jax.ShapeDtypeStruct
    sent = pl.pallas_call(
        messages_out,
        out_shape=shape((owners, SENT, slots), F32),
        in_specs=[HBM] * 7,
        out_specs=HBM,
        scratch_shapes=[
            pltpu.VMEM((FIELDS, FLAT, CY), F32),
            pltpu.VMEM((2, owners, slots), jnp.int32),
            pltpu.VMEM((owners, slots), F32),
            pltpu.VMEM((2, owners, slots), F32),
            pltpu.VMEM((owners, SENT, slots), F32),
            pltpu.VMEM((CY, CY), F32),
            pltpu.SemaphoreType.DMA((7,)),
        ],
        compiler_params=WHOLE,
        cost_estimate=cost(100000, 3000000),
    )(u, v, t, cells[0], levels[0], jnp.swapaxes(bary[0], 0, 1), vfrac[0])
    got = lax.all_to_all(sent, BOTH, split_axis=0, concat_axis=0, tiled=True)
    columns = shape((2 * BLOCKS, CY), F32)
    edge = shape((EDGE, CY), F32)
    own_a, own_b, row_a, row_b = pl.pallas_call(
        edges_out,
        out_shape=(columns, columns, edge, edge),
        in_specs=[VMEM] * 3,
        compiler_params=PARAMS,
        cost_estimate=cost(100000, 1000000),
    )(u, v, t)
    col_b = lax.ppermute(own_b, "py", swap("py", 1))
    col_a = lax.ppermute(own_a, "py", swap("py", 0))
    row_b = lax.ppermute(row_b, "px", swap("px", 1))
    row_a = lax.ppermute(row_a, "px", swap("px", 0))
    patch = shape((FLAT, CY), F32)
    plane = shape((LEV, CY), F32)
    grid = shape((24 * LEV, 2 * CY), BF16)
    turn = pltpu.VMEM((CY, CY), F32)
    u_part, v_part, t_part, pick = pl.pallas_call(
        bulk,
        out_shape=(patch, patch, patch, shape((4 * CY, 4 * CY), BF16)),
        in_specs=[VMEM] * 3 + [SMEM] * 2,
        compiler_params=PARAMS,
        cost_estimate=cost(8000000, 10000000),
    )(u, v, t, hyper, damp)
    across = pltpu.VMEM((8, CY), F32)
    t_most, table, coef, quarter = pl.pallas_call(
        theta_borders,
        out_shape=(patch, grid, plane, plane),
        in_specs=[VMEM] * 8 + [SMEM] * 2 + [VMEM],
        scratch_shapes=[turn, across],
        compiler_params=PARAMS,
        cost_estimate=cost(4000000, 3000000),
    )(u, t_part, own_a, own_b, col_b, col_a, row_a, row_b, hyper, damp, pick)
    _, model = pl.pallas_call(
        interpolate,
        out_shape=(grid, shape((owners, slots), F32)),
        in_specs=[VMEM] * 4,
        scratch_shapes=[pltpu.VMEM((owners, slots), jnp.int32)] * 4 + [turn],
        input_output_aliases={0: 0},
        compiler_params=PARAMS,
        cost_estimate=cost(6500000000, 1000000),
    )(table, got, t_most, coef)
    u_next, v_next, t_next = pl.pallas_call(
        rest,
        out_shape=(patch, patch, patch),
        in_specs=[VMEM] * 10 + [SMEM] * 2,
        scratch_shapes=[turn, across],
        compiler_params=PARAMS,
        cost_estimate=cost(4000000, 3000000),
    )(u_part, v_part, t_most, col_b, col_a, row_a, row_b, got, coef, quarter, hyper, damp)
    back = lax.all_to_all(model, BOTH, split_axis=0, concat_axis=0, tiled=True)
    departures = mask.astype(F32) * (values - back[None])
    whole = theta.shape
    return t_next.reshape(whole), u_next.reshape(whole), v_next.reshape(whole), departures


def solution(mesh):
    field = P(None, "px", "py")
    obs = P(BOTH, None, None)
    return jax.shard_map(
        on_device,
        mesh=mesh,
        in_specs=(field, field, field, P(), P(), obs, obs, P(BOTH, None, None, None), obs, obs, obs),
        out_specs=(field, field, field, obs),
        check_vma=False,
    )
```

```python
import jax
import jax.numpy as jnp
from jax import lax
from jax.experimental import pallas as pl
from jax.experimental.pallas import tpu as pltpu
from jax.sharding import PartitionSpec as P

LEV = 32
CX = 16
CY = 128
FLAT = LEV * CX
FIELDS = 3
OBS = 5
SENT = OBS + FIELDS
ROWS = (0, 1, CX - 2, CX - 1)
BLOCKS = FIELDS * FLAT // 128
EDGE = 2 * FIELDS * LEV
UNROLL = 32
BOTH = ("px", "py")
F32 = jnp.float32
BF16 = jnp.bfloat16
VMEM = pl.BlockSpec(memory_space=pltpu.VMEM)
SMEM = pl.BlockSpec(memory_space=pltpu.SMEM)
HBM = pl.BlockSpec(memory_space=pltpu.MemorySpace.HBM)
PARAMS = pltpu.CompilerParams(vmem_limit_bytes=48 << 20)


WHOLE = pltpu.CompilerParams(vmem_limit_bytes=60 << 20)


def cost(flops, moved):
    return pl.CostEstimate(flops=flops, bytes_accessed=moved, transcendentals=0)


def diagonal(move_x, move_y):
    count_x, count_y = lax.axis_size("px"), lax.axis_size("py")
    x = lax.rem(lax.axis_index("px") + count_x + move_x, count_x)
    return x * count_y + lax.rem(lax.axis_index("py") + count_y + move_y, count_y)


def messages_out(u, v, t, cells, levels, bary, vfrac, sent, fields, ints, packed, turn, sems):
    copies = [
        pltpu.make_async_copy(u, fields.at[0], sems.at[0]),
        pltpu.make_async_copy(v, fields.at[1], sems.at[1]),
        pltpu.make_async_copy(t, fields.at[2], sems.at[2]),
        pltpu.make_async_copy(cells, ints.at[0], sems.at[3]),
        pltpu.make_async_copy(levels, ints.at[1], sems.at[4]),
        pltpu.make_async_copy(vfrac, packed.at[:, 2, :], sems.at[5]),
        pltpu.make_async_copy(bary.at[0], packed.at[:, 3, :], sems.at[6]),
        pltpu.make_async_copy(bary.at[1], packed.at[:, 4, :], sems.at[7]),
    ]
    for copy in copies:
        copy.start()
    packed[:, OBS:, :] = jnp.zeros((packed.shape[0], FIELDS, CY), F32)
    for copy in copies:
        copy.wait()
    packed[:, 0, :] = ints[0].astype(F32)
    packed[:, 1, :] = ints[1].astype(F32)
    half = lax.broadcasted_iota(jnp.int32, (1, CY), 1) < CY // 2
    for f in range(FIELDS):
        for i, r in enumerate(ROWS):
            turn[i * LEV : (i + 1) * LEV, :] = fields[f, pl.ds(r, LEV, stride=CX), :]
        turned = turn[...].T
        for move_y, c in ((-1, 0), (1, CY - 2)):
            one, two = turned[c : c + 1, :], turned[c + 1 : c + 2, :]
            row = OBS + f
            packed[diagonal(-1, move_y), row : row + 1, :] = jnp.where(
                half, one, pltpu.roll(two, CY // 2, 1)
            )
            packed[diagonal(1, move_y), row : row + 1, :] = jnp.where(
                half, pltpu.roll(one, CY // 2, 1), two
            )
    pltpu.sync_copy(packed, sent)


def is_even(axis):
    return lax.rem(lax.axis_index(axis), 2) == 0


def edges_out(u, v, t, col_a, col_b, row_a, row_b):
    even_x, even_y = is_even("px"), is_even("py")
    for f, field in enumerate((u, v, t)):
        for i in range(2):
            at = (i * FIELDS + f) * LEV
            low = field[pl.ds(i, LEV, stride=CX), :]
            high = field[pl.ds(CX - 2 + i, LEV, stride=CX), :]
            row_a[at : at + LEV, :] = jnp.where(even_x, high, low)
            row_b[at : at + LEV, :] = jnp.where(even_x, low, high)
        for k in range(FLAT // 128):
            turned = field[k * 128 : (k + 1) * 128, :].T
            first, last = turned[0:2, :], turned[CY - 2 :, :]
            at = 2 * (f * FLAT // 128 + k)
            col_a[at : at + 2, :] = jnp.where(even_y, last, first)
            col_b[at : at + 2, :] = jnp.where(even_y, first, last)


def shifted(lane, field, border, b):
    if b > 0:
        return pltpu.roll(jnp.where(lane < b, border, field), CY - b, 1)
    return pltpu.roll(jnp.where(lane >= CY + b, border, field), -b, 1)


def per_level(coef, quarter, hyper, damp):
    for lev in range(LEV):
        coef[lev : lev + 1, :] = jnp.full((1, CY), hyper[lev], F32)
        quarter[lev : lev + 1, :] = jnp.full((1, CY), damp[lev] * 0.25, F32)


def one(line, sign):
    c, e1, e2, w1, w2 = line
    if sign > 0:
        return 2.0 * (e1 + w2) - 10.0 * (c + w1)
    return 2.0 * (w1 + e2) - 10.0 * (c + e1)


def two(line, sign):
    c, e1, e2, w1, w2 = line
    return c + w2 + 2.0 * w1 if sign > 0 else c + e2 + 2.0 * e1


def add(out, r, value):
    out[pl.ds(r, LEV, stride=CX), :] += value


def border_rows(sign):
    return (CX - 1, CX - 2) if sign > 0 else (0, 1)


def add_theta_rows(t_out, near, far, sign, k4, wind):
    edge, following = border_rows(sign)
    add(t_out, edge, -k4 * (one(near, sign) + two(far, sign)) - (0.25 * sign) * wind * near[0])
    add(t_out, following, -k4 * two(near, sign))


def add_wind_rows(u_out, v_out, near, far, sign, k4, k2):
    edge, following = border_rows(sign)
    (u1, v1), (u2, v2) = near, far
    add(u_out, edge, k2 * (u2[0] + sign * (v1[1] - v1[3])) - k4 * (one(u1, sign) + two(u2, sign)))
    add(u_out, following, k2 * u1[0] - k4 * two(u1, sign))
    add(v_out, edge, k2 * (sign * (u1[1] - u1[3])) - k4 * (one(v1, sign) + two(v2, sign)))
    add(v_out, following, -k4 * two(v1, sign))


def bulk(u, v, t, hyper, damp, u_out, v_out, t_out, pick):
    lane = lax.broadcasted_iota(jnp.int32, (CX, CY), 1)
    none = jnp.zeros((8, CY), F32)

    def rows(value, a):
        return pltpu.roll(jnp.concatenate([value, none], axis=0), -a % (CX + 8), 0)[:CX, :]

    def level(lev, carry):
        coef = hyper[lev]
        quarter = damp[lev] * 0.25
        at = pl.multiple_of(lev * CX, 8)
        views = []
        fourth = []
        for field in (u, v, t):
            c = field[pl.ds(at, CX), :]
            e1, e2, w1, w2 = (shifted(lane, c, 0.0, b) for b in (1, 2, -1, -2))
            total = 42.0 * c - 10.0 * (e1 + w1) + (e2 + w2)
            total = total + rows(2.0 * (e1 + w2) - 10.0 * (c + w1), 1)
            total = total + rows(2.0 * (w1 + e2) - 10.0 * (c + e1), -1)
            total = total + rows(c + w2 + 2.0 * w1, 2) + rows(c + e2 + 2.0 * e1, -2)
            fourth.append(total)
            views.append((c, e1, w1, e2, w2))
        (u0, ue, uw, _, _), (v0, ve, vw, ve2, vw2), (t0, te, tw, _, _) = views
        du, dv = ue - uw, ve - vw
        uxx = rows(u0, 2) - 2.0 * u0 + rows(u0, -2)
        vxy = rows(dv, 1) - rows(dv, -1)
        uxy = rows(du, 1) - rows(du, -1)
        vyy = ve2 - 2.0 * v0 + vw2
        u_out[pl.ds(at, CX), :] = u0 - coef * fourth[0] + quarter * (uxx + vxy)
        v_out[pl.ds(at, CX), :] = v0 - coef * fourth[1] + quarter * (uxy + vyy)
        drift = u0 * (rows(t0, 1) - rows(t0, -1)) + v0 * (te - tw)
        t_out[pl.ds(at, CX), :] = t0 - coef * fourth[2] - 0.25 * drift
        return carry

    lax.fori_loop(0, LEV, level, 0, unroll=4)
    k = lax.broadcasted_iota(jnp.int32, pick.shape, 0)
    n = lax.broadcasted_iota(jnp.int32, pick.shape, 1)
    want = ((n >> 5) & 3) * CY + (n & 31) * 4 + (n >> 7)
    pick[...] = jnp.where(k == want, 1.0, 0.0).astype(BF16)


def level_rows(across, hyper, damp):
    parts = FLAT // 128
    spot = lax.broadcasted_iota(jnp.int32, (1, CY), 1) >> 4
    for k in range(parts):
        c, q = jnp.zeros((1, CY), F32), jnp.zeros((1, CY), F32)
        for i in range(8):
            c = jnp.where(spot == i, hyper[8 * k + i], c)
            q = jnp.where(spot == i, damp[8 * k + i] * 0.25, q)
        across[k : k + 1, :] = c
        across[parts + k : parts + k + 1, :] = q
    return across[0:parts, :], across[parts : 2 * parts, :]


def line(yes, no, keep, f, col):
    parts = FLAT // 128
    at = pl.ds(2 * parts * f + col, parts, stride=2)
    return jnp.where(keep, yes[at, :], no[at, :])


def beside(col_a, col_b, keep, f):
    east = [line(col_a, col_b, keep, f, i) for i in range(2)]
    west = [line(col_b, col_a, keep, f, i) for i in (1, 0)]
    return east, west


def moved(x, a):
    place = lax.broadcasted_iota(jnp.int32, x.shape, 1) & (CX - 1)
    inside = place < CX - a if a > 0 else place >= -a
    return jnp.where(inside, pltpu.roll(x, -a % CY, 1), 0.0)


def next_one(x, s):
    return x + 2.0 * moved(x, -s) + moved(x, -2 * s)


def nearest(x, y, s):
    total = 2.0 * moved(x, s) - 10.0 * (x + moved(x, -s)) + 2.0 * moved(x, -2 * s)
    return total + next_one(y, s)


def slope(x):
    return moved(x, 1) - moved(x, -1)


def add_columns(start, out, terms, turn):
    for k in range(FLAT // 128):
        for col, term in zip((0, 1, CY - 2, CY - 1), terms):
            turn[col : col + 1, :] = term[k : k + 1, :]
        out[k * 128 : (k + 1) * 128, :] = start[k * 128 : (k + 1) * 128, :] + turn[...].T


def outside(this, other, keep, f, i):
    lane = lax.broadcasted_iota(jnp.int32, (LEV, CY), 1)
    at = (i * FIELDS + f) * LEV
    c = jnp.where(keep, this[at : at + LEV, :], other[at : at + LEV, :])
    return (c,) + tuple(shifted(lane, c, 0.0, b) for b in (1, 2, -1, -2))


def theta_borders(
    u, t_in, own_a, own_b, col_b, col_a, row_a, row_b, hyper, damp, pick, t_out, table, coef, quarter, turn, across
):
    even_x, even_y = is_even("px"), is_even("py")
    per_level(coef, quarter, hyper, damp)
    c4, _ = level_rows(across, hyper, damp)
    east, west = beside(col_a, col_b, even_y, 2)
    v_first, v_last = line(own_b, own_a, even_y, 1, 0), line(own_a, own_b, even_y, 1, 1)
    turn[...] = jnp.zeros_like(turn)
    terms = (
        -c4 * nearest(*west, -1) + 0.25 * v_first * west[0],
        -c4 * next_one(west[0], -1),
        -c4 * next_one(east[0], 1),
        -c4 * nearest(*east, 1) - 0.25 * v_last * east[0],
    )
    add_columns(t_in, t_out, terms, turn)
    for sign, this, other, near, far in ((-1, row_b, row_a, 1, 0), (1, row_a, row_b, 0, 1)):
        wind = u[pl.ds(border_rows(sign)[0], LEV, stride=CX), :]
        near, far = (outside(this, other, even_x, 2, i) for i in (near, far))
        add_theta_rows(t_out, near, far, sign, coef[...], wind)
    both = []
    for rl in range(4):
        parts = [t_out[pl.ds(4 * rh + rl, LEV, stride=CX), :] for rh in range(4)]
        tops = [part.astype(BF16) for part in parts]
        rests = [(part - top.astype(F32)).astype(BF16) for part, top in zip(parts, tops)]
        both += [jnp.concatenate(tops, axis=1), jnp.concatenate(rests, axis=1)]
    put = jnp.dot(jnp.concatenate(both, axis=0), pick[...], preferred_element_type=F32)
    for rl in range(4):
        for half in range(2):
            lanes = slice(half * 128, half * 128 + 128)
            for cl in range(4):
                at = (2 * rl + half) * LEV
                x = put[at : at + LEV, cl * 128 : (cl + 1) * 128]
                table[(rl * 5 + cl) * LEV : (rl * 5 + cl + 1) * LEV, lanes] = x.astype(BF16)
                if cl == 0:
                    table[(rl * 5 + 4) * LEV : (rl * 5 + 5) * LEV, lanes] = pltpu.roll(
                        x, 127, 1
                    ).astype(BF16)
                if rl == 0:
                    table[(20 + cl) * LEV : (21 + cl) * LEV, lanes] = pltpu.roll(x, 96, 1).astype(BF16)


def corner_lines(obs, turn, f):
    turn[...] = jnp.zeros_like(turn)
    row = OBS + f
    half = lax.broadcasted_iota(jnp.int32, (1, CY), 1) < CY // 2
    for move_y, c in ((1, 0), (-1, CY - 2)):
        upper = obs[diagonal(-1, move_y), row : row + 1, :]
        lower = obs[diagonal(1, move_y), row : row + 1, :]
        turn[c : c + 1, :] = jnp.where(half, upper, pltpu.roll(lower, CY // 2, 1))
        turn[c + 1 : c + 2, :] = jnp.where(half, pltpu.roll(upper, CY // 2, 1), lower)
    spots = turn[...].T
    lane = lax.broadcasted_iota(jnp.int32, (LEV, CY), 1)
    none = jnp.zeros((LEV, CY), F32)
    lines = []
    for i in range(4):
        h = spots[i * LEV : (i + 1) * LEV, :]
        lines.append((none,) + tuple(shifted(lane, none, h, b) for b in (1, 2, -1, -2)))
    return lines


def rest(
    u_in, v_in, t_in, col_b, col_a, row_a, row_b, obs, coef, quarter, hyper, damp, u_out, v_out, t_out, turn, across
):
    even_x, even_y = is_even("px"), is_even("py")
    c4, q4 = level_rows(across, hyper, damp)
    ue, uw = beside(col_a, col_b, even_y, 0)
    ve, vw = beside(col_a, col_b, even_y, 1)
    turn[...] = jnp.zeros_like(turn)
    add_columns(
        u_in,
        u_out,
        (
            -c4 * nearest(*uw, -1) - q4 * slope(vw[0]),
            -c4 * next_one(uw[0], -1),
            -c4 * next_one(ue[0], 1),
            -c4 * nearest(*ue, 1) + q4 * slope(ve[0]),
        ),
        turn,
    )
    add_columns(
        v_in,
        v_out,
        (
            -c4 * nearest(*vw, -1) + q4 * (vw[1] - slope(uw[0])),
            -c4 * next_one(vw[0], -1) + q4 * vw[0],
            -c4 * next_one(ve[0], 1) + q4 * ve[0],
            -c4 * nearest(*ve, 1) + q4 * (ve[1] + slope(ue[0])),
        ),
        turn,
    )
    t_out[...] = t_in[...]
    lines = [corner_lines(obs, turn, f) for f in range(FIELDS)]
    none = jnp.zeros((LEV, CY), F32)
    for sign, this, other, near, far in ((-1, row_b, row_a, 1, 0), (1, row_a, row_b, 0, 1)):
        spot = 0 if sign < 0 else 2
        straight = [[outside(this, other, even_x, f, i) for f in range(2)] for i in (near, far)]
        corner = [[lines[f][spot + i] for f in range(FIELDS)] for i in (near, far)]
        both = [
            [tuple(p + q for p, q in zip(straight[i][f], corner[i][f])) for f in range(2)] for i in range(2)
        ]
        add_wind_rows(u_out, v_out, both[0], both[1], sign, coef[...], quarter[...])
        add_theta_rows(t_out, corner[0][2], corner[1][2], sign, coef[...], none)


def interpolate(start, obs, t, coef, table, model, block, row, col, lev, turn):
    far_up, near_up, near_down, far_down = corner_lines(obs, turn, 2)
    terms = (
        one(near_up, -1) + two(far_up, -1),
        two(near_up, -1),
        two(near_down, 1),
        one(near_down, 1) + two(far_down, 1),
    )
    lane = lax.broadcasted_iota(jnp.int32, (LEV, CY), 1)
    for r, term in zip(ROWS, terms):
        value = t[pl.ds(r, LEV, stride=CX), :] - coef[...] * term
        for c in (0, 1, CY - 2, CY - 1):
            to = (r >> 2) * 32 + (c >> 2)
            moved = pltpu.roll(value, (to - c) % CY, 1)
            high = moved.astype(BF16).astype(F32)
            at = ((r & 3) * 5 + (c & 3)) * LEV
            for k, part in enumerate((high, moved - high)):
                old = start[at : at + LEV, k * CY : (k + 1) * CY].astype(F32)
                table[at : at + LEV, k * CY : (k + 1) * CY] = jnp.where(lane == to, part, old).astype(BF16)
    owners = model.shape[0]
    cell = obs[:, 0, :].astype(jnp.int32)
    c, r = cell & (CY - 1), cell >> 7
    block[...] = (r >> 2) * 32 + (c >> 2)
    row[...] = r & 3
    col[...] = c & 3
    lev[...] = obs[:, 1, :].astype(jnp.int32)
    wide = 256
    block_iota = lax.broadcasted_iota(jnp.int32, (128, wide), 0)
    lev_iota = lax.broadcasted_iota(jnp.int32, (LEV, wide), 0)

    def pair(p, carry):
        def two(ref):
            return jnp.concatenate([ref[pl.ds(2 * p, 1), :], ref[pl.ds(2 * p + 1, 1), :]], axis=1)

        def sent(k):
            return jnp.concatenate([obs[2 * p, k : k + 1, :], obs[2 * p + 1, k : k + 1, :]], axis=1)

        def bit(value, mask):
            return jnp.broadcast_to(value & mask, (LEV, wide)) != 0

        at, r, c, l = two(block), two(row), two(col), two(lev)
        a, w0, w1 = sent(2), sent(3), sent(4)
        w2 = 1.0 - w0 - w1
        hot = jnp.where(block_iota == at, 1.0, 0.0).astype(BF16)
        got = jnp.dot(
            table[...], jnp.concatenate([hot, hot], axis=0), preferred_element_type=F32
        )
        c1, c2, r1, r2 = bit(c, 1), bit(c, 2), bit(r, 1), bit(r, 2)
        here, beside = [], []
        for i in range(5):
            g = [got[(i * 5 + j) * LEV : (i * 5 + j + 1) * LEV, :] for j in range(5 if i < 4 else 4)]
            h1 = jnp.where(c2, g[3], g[1])
            here.append(jnp.where(c1, h1, jnp.where(c2, g[2], g[0])))
            if i < 4:
                beside.append(jnp.where(c1, jnp.where(c2, g[4], g[2]), h1))
        h0, h1, h2 = (jnp.where(r2, here[i + 2], here[i]) for i in range(3))
        t0, t1 = jnp.where(r1, h1, h0), jnp.where(r1, h2, h1)
        t2 = jnp.where(
            r1, jnp.where(r2, beside[3], beside[1]), jnp.where(r2, beside[2], beside[0])
        )
        weight = jnp.where(lev_iota == l, 1.0 - a, jnp.where(lev_iota == l + 1, a, 0.0))
        out = jnp.sum(weight * (w0 * t0 + w1 * t1 + w2 * t2), axis=0, keepdims=True)
        model[pl.ds(2 * p, 1), :] = out[:, :128]
        model[pl.ds(2 * p + 1, 1), :] = out[:, 128:]
        return carry

    lax.fori_loop(0, owners // 2, pair, 0, unroll=UNROLL)


def swap(axis, first):
    count = lax.axis_size(axis)
    pairs = [((i + first) % count, (i + first + 1) % count) for i in range(0, count, 2)]
    return pairs + [(b, a) for a, b in pairs]


def on_device(theta, wind_u, wind_v, hyper, damp, cells, levels, bary, vfrac, values, mask):
    u, v, t = (f.reshape(FLAT, CY) for f in (wind_u, wind_v, theta))
    owners, slots = cells.shape[1], cells.shape[2]
    shape = jax.ShapeDtypeStruct
    sent = pl.pallas_call(
        messages_out,
        out_shape=shape((owners, SENT, slots), F32),
        in_specs=[HBM] * 7,
        out_specs=HBM,
        scratch_shapes=[
            pltpu.VMEM((FIELDS, FLAT, CY), F32),
            pltpu.VMEM((2, owners, slots), jnp.int32),
            pltpu.VMEM((owners, SENT, slots), F32),
            pltpu.VMEM((CY, CY), F32),
            pltpu.SemaphoreType.DMA((8,)),
        ],
        compiler_params=WHOLE,
        cost_estimate=cost(100000, 3000000),
    )(u, v, t, cells[0], levels[0], jnp.swapaxes(bary[0], 0, 1), vfrac[0])
    got = lax.all_to_all(sent, BOTH, split_axis=0, concat_axis=0, tiled=True)
    columns = shape((2 * BLOCKS, CY), F32)
    edge = shape((EDGE, CY), F32)
    own_a, own_b, row_a, row_b = pl.pallas_call(
        edges_out,
        out_shape=(columns, columns, edge, edge),
        in_specs=[VMEM] * 3,
        compiler_params=PARAMS,
        cost_estimate=cost(100000, 1000000),
    )(u, v, t)
    col_b = lax.ppermute(own_b, "py", swap("py", 1))
    col_a = lax.ppermute(own_a, "py", swap("py", 0))
    row_b = lax.ppermute(row_b, "px", swap("px", 1))
    row_a = lax.ppermute(row_a, "px", swap("px", 0))
    patch = shape((FLAT, CY), F32)
    plane = shape((LEV, CY), F32)
    grid = shape((24 * LEV, 2 * CY), BF16)
    turn = pltpu.VMEM((CY, CY), F32)
    u_part, v_part, t_part, pick = pl.pallas_call(
        bulk,
        out_shape=(patch, patch, patch, shape((4 * CY, 4 * CY), BF16)),
        in_specs=[VMEM] * 3 + [SMEM] * 2,
        compiler_params=PARAMS,
        cost_estimate=cost(8000000, 10000000),
    )(u, v, t, hyper, damp)
    across = pltpu.VMEM((8, CY), F32)
    t_most, table, coef, quarter = pl.pallas_call(
        theta_borders,
        out_shape=(patch, grid, plane, plane),
        in_specs=[VMEM] * 8 + [SMEM] * 2 + [VMEM],
        scratch_shapes=[turn, across],
        compiler_params=PARAMS,
        cost_estimate=cost(4000000, 3000000),
    )(u, t_part, own_a, own_b, col_b, col_a, row_a, row_b, hyper, damp, pick)
    _, model = pl.pallas_call(
        interpolate,
        out_shape=(grid, shape((owners, slots), F32)),
        in_specs=[VMEM] * 4,
        scratch_shapes=[pltpu.VMEM((owners, slots), jnp.int32)] * 4 + [turn],
        input_output_aliases={0: 0},
        compiler_params=PARAMS,
        cost_estimate=cost(6500000000, 1000000),
    )(table, got, t_most, coef)
    u_next, v_next, t_next = pl.pallas_call(
        rest,
        out_shape=(patch, patch, patch),
        in_specs=[VMEM] * 10 + [SMEM] * 2,
        scratch_shapes=[turn, across],
        compiler_params=PARAMS,
        cost_estimate=cost(4000000, 3000000),
    )(u_part, v_part, t_most, col_b, col_a, row_a, row_b, got, coef, quarter, hyper, damp)
    back = lax.all_to_all(model, BOTH, split_axis=0, concat_axis=0, tiled=True)
    departures = mask.astype(F32) * (values - back[None])
    whole = theta.shape
    return t_next.reshape(whole), u_next.reshape(whole), v_next.reshape(whole), departures


def solution(mesh):
    field = P(None, "px", "py")
    obs = P(BOTH, None, None)
    return jax.shard_map(
        on_device,
        mesh=mesh,
        in_specs=(field, field, field, P(), P(), obs, obs, P(BOTH, None, None, None), obs, obs, obs),
        out_specs=(field, field, field, obs),
        check_vma=False,
    )
```

```python
import jax
import jax.numpy as jnp
from jax import lax
from jax.experimental import pallas as pl
from jax.experimental.pallas import tpu as pltpu
from jax.sharding import PartitionSpec as P

LEV = 32
CX = 16
CY = 128
FLAT = LEV * CX
FIELDS = 3
OBS = 5
SENT = OBS + FIELDS
ROWS = (0, 1, CX - 2, CX - 1)
BLOCKS = FIELDS * FLAT // 128
EDGE = 2 * FIELDS * LEV
UNROLL = 32
BOTH = ("px", "py")
F32 = jnp.float32
BF16 = jnp.bfloat16
VMEM = pl.BlockSpec(memory_space=pltpu.VMEM)
SMEM = pl.BlockSpec(memory_space=pltpu.SMEM)
HBM = pl.BlockSpec(memory_space=pltpu.MemorySpace.HBM)
PARAMS = pltpu.CompilerParams(vmem_limit_bytes=48 << 20)


WHOLE = pltpu.CompilerParams(vmem_limit_bytes=60 << 20)


def cost(flops, moved):
    return pl.CostEstimate(flops=flops, bytes_accessed=moved, transcendentals=0)


def diagonal(move_x, move_y):
    count_x, count_y = lax.axis_size("px"), lax.axis_size("py")
    x = lax.rem(lax.axis_index("px") + count_x + move_x, count_x)
    return x * count_y + lax.rem(lax.axis_index("py") + count_y + move_y, count_y)


def messages_out(u, v, t, cells, levels, bary, vfrac, sent, fields, ints, packed, turn, sems):
    copies = [
        pltpu.make_async_copy(u, fields.at[0], sems.at[0]),
        pltpu.make_async_copy(v, fields.at[1], sems.at[1]),
        pltpu.make_async_copy(t, fields.at[2], sems.at[2]),
        pltpu.make_async_copy(cells, ints.at[0], sems.at[3]),
        pltpu.make_async_copy(levels, ints.at[1], sems.at[4]),
        pltpu.make_async_copy(vfrac, packed.at[:, 2, :], sems.at[5]),
        pltpu.make_async_copy(bary.at[0], packed.at[:, 3, :], sems.at[6]),
        pltpu.make_async_copy(bary.at[1], packed.at[:, 4, :], sems.at[7]),
    ]
    for copy in copies:
        copy.start()
    packed[:, OBS:, :] = jnp.zeros((packed.shape[0], FIELDS, CY), F32)
    for copy in copies:
        copy.wait()
    packed[:, 0, :] = ints[0].astype(F32)
    packed[:, 1, :] = ints[1].astype(F32)
    half = lax.broadcasted_iota(jnp.int32, (1, CY), 1) < CY // 2
    for f in range(FIELDS):
        for i, r in enumerate(ROWS):
            turn[i * LEV : (i + 1) * LEV, :] = fields[f, pl.ds(r, LEV, stride=CX), :]
        turned = turn[...].T
        for move_y, c in ((-1, 0), (1, CY - 2)):
            one, two = turned[c : c + 1, :], turned[c + 1 : c + 2, :]
            row = OBS + f
            packed[diagonal(-1, move_y), row : row + 1, :] = jnp.where(
                half, one, pltpu.roll(two, CY // 2, 1)
            )
            packed[diagonal(1, move_y), row : row + 1, :] = jnp.where(
                half, pltpu.roll(one, CY // 2, 1), two
            )
    pltpu.sync_copy(packed, sent)


def is_even(axis):
    return lax.rem(lax.axis_index(axis), 2) == 0


def edges_out(u, v, t, col_a, col_b, row_a, row_b):
    even_x, even_y = is_even("px"), is_even("py")
    for f, field in enumerate((u, v, t)):
        for i in range(2):
            at = (i * FIELDS + f) * LEV
            low = field[pl.ds(i, LEV, stride=CX), :]
            high = field[pl.ds(CX - 2 + i, LEV, stride=CX), :]
            row_a[at : at + LEV, :] = jnp.where(even_x, high, low)
            row_b[at : at + LEV, :] = jnp.where(even_x, low, high)
        for k in range(FLAT // 128):
            turned = field[k * 128 : (k + 1) * 128, :].T
            first, last = turned[0:2, :], turned[CY - 2 :, :]
            at = 2 * (f * FLAT // 128 + k)
            col_a[at : at + 2, :] = jnp.where(even_y, last, first)
            col_b[at : at + 2, :] = jnp.where(even_y, first, last)


def shifted(lane, field, border, b):
    if b > 0:
        return pltpu.roll(jnp.where(lane < b, border, field), CY - b, 1)
    return pltpu.roll(jnp.where(lane >= CY + b, border, field), -b, 1)


def per_level(coef, quarter, hyper, damp):
    for lev in range(LEV):
        coef[lev : lev + 1, :] = jnp.full((1, CY), hyper[lev], F32)
        quarter[lev : lev + 1, :] = jnp.full((1, CY), damp[lev] * 0.25, F32)


def one(line, sign):
    c, e1, e2, w1, w2 = line
    if sign > 0:
        return 2.0 * (e1 + w2) - 10.0 * (c + w1)
    return 2.0 * (w1 + e2) - 10.0 * (c + e1)


def two(line, sign):
    c, e1, e2, w1, w2 = line
    return c + w2 + 2.0 * w1 if sign > 0 else c + e2 + 2.0 * e1


def add(out, r, value):
    out[pl.ds(r, LEV, stride=CX), :] += value


def border_rows(sign):
    return (CX - 1, CX - 2) if sign > 0 else (0, 1)


def add_theta_rows(t_out, near, far, sign, k4, wind):
    edge, following = border_rows(sign)
    add(t_out, edge, -k4 * (one(near, sign) + two(far, sign)) - (0.25 * sign) * wind * near[0])
    add(t_out, following, -k4 * two(near, sign))


def add_wind_rows(u_out, v_out, near, far, sign, k4, k2):
    edge, following = border_rows(sign)
    (u1, v1), (u2, v2) = near, far
    add(u_out, edge, k2 * (u2[0] + sign * (v1[1] - v1[3])) - k4 * (one(u1, sign) + two(u2, sign)))
    add(u_out, following, k2 * u1[0] - k4 * two(u1, sign))
    add(v_out, edge, k2 * (sign * (u1[1] - u1[3])) - k4 * (one(v1, sign) + two(v2, sign)))
    add(v_out, following, -k4 * two(v1, sign))


def bulk(u, v, t, hyper, damp, u_out, v_out, t_out, pick, coef_out, quarter_out, across):
    per_level(coef_out, quarter_out, hyper, damp)
    level_rows(across, hyper, damp)
    lane = lax.broadcasted_iota(jnp.int32, (CX, CY), 1)
    none = jnp.zeros((8, CY), F32)

    def rows(value, a):
        return pltpu.roll(jnp.concatenate([value, none], axis=0), -a % (CX + 8), 0)[:CX, :]

    def level(lev, carry):
        coef = hyper[lev]
        quarter = damp[lev] * 0.25
        at = pl.multiple_of(lev * CX, 8)
        views = []
        fourth = []
        for field in (u, v, t):
            c = field[pl.ds(at, CX), :]
            e1, e2, w1, w2 = (shifted(lane, c, 0.0, b) for b in (1, 2, -1, -2))
            total = 42.0 * c - 10.0 * (e1 + w1) + (e2 + w2)
            total = total + rows(2.0 * (e1 + w2) - 10.0 * (c + w1), 1)
            total = total + rows(2.0 * (w1 + e2) - 10.0 * (c + e1), -1)
            total = total + rows(c + w2 + 2.0 * w1, 2) + rows(c + e2 + 2.0 * e1, -2)
            fourth.append(total)
            views.append((c, e1, w1, e2, w2))
        (u0, ue, uw, _, _), (v0, ve, vw, ve2, vw2), (t0, te, tw, _, _) = views
        du, dv = ue - uw, ve - vw
        uxx = rows(u0, 2) - 2.0 * u0 + rows(u0, -2)
        vxy = rows(dv, 1) - rows(dv, -1)
        uxy = rows(du, 1) - rows(du, -1)
        vyy = ve2 - 2.0 * v0 + vw2
        u_out[pl.ds(at, CX), :] = u0 - coef * fourth[0] + quarter * (uxx + vxy)
        v_out[pl.ds(at, CX), :] = v0 - coef * fourth[1] + quarter * (uxy + vyy)
        drift = u0 * (rows(t0, 1) - rows(t0, -1)) + v0 * (te - tw)
        t_out[pl.ds(at, CX), :] = t0 - coef * fourth[2] - 0.25 * drift
        return carry

    lax.fori_loop(0, LEV, level, 0, unroll=4)
    k = lax.broadcasted_iota(jnp.int32, pick.shape, 0)
    n = lax.broadcasted_iota(jnp.int32, pick.shape, 1)
    want = ((n >> 5) & 3) * CY + (n & 31) * 4 + (n >> 7)
    pick[...] = jnp.where(k == want, 1.0, 0.0).astype(BF16)


def level_rows(across, hyper, damp):
    parts = FLAT // 128
    spot = lax.broadcasted_iota(jnp.int32, (1, CY), 1) >> 4
    for k in range(parts):
        c, q = jnp.zeros((1, CY), F32), jnp.zeros((1, CY), F32)
        for i in range(8):
            c = jnp.where(spot == i, hyper[8 * k + i], c)
            q = jnp.where(spot == i, damp[8 * k + i] * 0.25, q)
        across[k : k + 1, :] = c
        across[parts + k : parts + k + 1, :] = q


def line(yes, no, keep, f, col):
    parts = FLAT // 128
    at = pl.ds(2 * parts * f + col, parts, stride=2)
    return jnp.where(keep, yes[at, :], no[at, :])


def beside(col_a, col_b, keep, f):
    east = [line(col_a, col_b, keep, f, i) for i in range(2)]
    west = [line(col_b, col_a, keep, f, i) for i in (1, 0)]
    return east, west


def moved(x, a):
    place = lax.broadcasted_iota(jnp.int32, x.shape, 1) & (CX - 1)
    inside = place < CX - a if a > 0 else place >= -a
    return jnp.where(inside, pltpu.roll(x, -a % CY, 1), 0.0)


def next_one(x, s):
    return x + 2.0 * moved(x, -s) + moved(x, -2 * s)


def nearest(x, y, s):
    total = 2.0 * moved(x, s) - 10.0 * (x + moved(x, -s)) + 2.0 * moved(x, -2 * s)
    return total + next_one(y, s)


def slope(x):
    return moved(x, 1) - moved(x, -1)


def add_columns(start, out, terms, turn):
    for k in range(FLAT // 128):
        for col, term in zip((0, 1, CY - 2, CY - 1), terms):
            turn[col : col + 1, :] = term[k : k + 1, :]
        out[k * 128 : (k + 1) * 128, :] = start[k * 128 : (k + 1) * 128, :] + turn[...].T


def outside(this, other, keep, f, i):
    lane = lax.broadcasted_iota(jnp.int32, (LEV, CY), 1)
    at = (i * FIELDS + f) * LEV
    c = jnp.where(keep, this[at : at + LEV, :], other[at : at + LEV, :])
    return (c,) + tuple(shifted(lane, c, 0.0, b) for b in (1, 2, -1, -2))


def theta_borders(
    u, t_in, own_a, own_b, col_b, col_a, row_a, row_b, pick, coef, across, t_out, table, turn
):
    even_x, even_y = is_even("px"), is_even("py")
    c4 = across[0 : FLAT // 128, :]
    east, west = beside(col_a, col_b, even_y, 2)
    v_first, v_last = line(own_b, own_a, even_y, 1, 0), line(own_a, own_b, even_y, 1, 1)
    turn[...] = jnp.zeros_like(turn)
    terms = (
        -c4 * nearest(*west, -1) + 0.25 * v_first * west[0],
        -c4 * next_one(west[0], -1),
        -c4 * next_one(east[0], 1),
        -c4 * nearest(*east, 1) - 0.25 * v_last * east[0],
    )
    add_columns(t_in, t_out, terms, turn)
    for sign, this, other, near, far in ((-1, row_b, row_a, 1, 0), (1, row_a, row_b, 0, 1)):
        wind = u[pl.ds(border_rows(sign)[0], LEV, stride=CX), :]
        near, far = (outside(this, other, even_x, 2, i) for i in (near, far))
        add_theta_rows(t_out, near, far, sign, coef[...], wind)
    both = []
    for rl in range(4):
        parts = [t_out[pl.ds(4 * rh + rl, LEV, stride=CX), :] for rh in range(4)]
        tops = [part.astype(BF16) for part in parts]
        rests = [(part - top.astype(F32)).astype(BF16) for part, top in zip(parts, tops)]
        both += [jnp.concatenate(tops, axis=1), jnp.concatenate(rests, axis=1)]
    put = jnp.dot(jnp.concatenate(both, axis=0), pick[...], preferred_element_type=F32)
    for rl in range(4):
        for half in range(2):
            lanes = slice(half * 128, half * 128 + 128)
            for cl in range(4):
                at = (2 * rl + half) * LEV
                x = put[at : at + LEV, cl * 128 : (cl + 1) * 128]
                table[(rl * 5 + cl) * LEV : (rl * 5 + cl + 1) * LEV, lanes] = x.astype(BF16)
                if cl == 0:
                    table[(rl * 5 + 4) * LEV : (rl * 5 + 5) * LEV, lanes] = pltpu.roll(
                        x, 127, 1
                    ).astype(BF16)
                if rl == 0:
                    table[(20 + cl) * LEV : (21 + cl) * LEV, lanes] = pltpu.roll(x, 96, 1).astype(BF16)


def corner_lines(obs, turn, f):
    turn[...] = jnp.zeros_like(turn)
    row = OBS + f
    half = lax.broadcasted_iota(jnp.int32, (1, CY), 1) < CY // 2
    for move_y, c in ((1, 0), (-1, CY - 2)):
        upper = obs[diagonal(-1, move_y), row : row + 1, :]
        lower = obs[diagonal(1, move_y), row : row + 1, :]
        turn[c : c + 1, :] = jnp.where(half, upper, pltpu.roll(lower, CY // 2, 1))
        turn[c + 1 : c + 2, :] = jnp.where(half, pltpu.roll(upper, CY // 2, 1), lower)
    spots = turn[...].T
    lane = lax.broadcasted_iota(jnp.int32, (LEV, CY), 1)
    none = jnp.zeros((LEV, CY), F32)
    lines = []
    for i in range(4):
        h = spots[i * LEV : (i + 1) * LEV, :]
        lines.append((none,) + tuple(shifted(lane, none, h, b) for b in (1, 2, -1, -2)))
    return lines


def rest(
    u_in, v_in, t_in, col_b, col_a, row_a, row_b, obs, coef, quarter, across, u_out, v_out, t_out, turn
):
    even_x, even_y = is_even("px"), is_even("py")
    c4, q4 = across[0 : FLAT // 128, :], across[FLAT // 128 :, :]
    ue, uw = beside(col_a, col_b, even_y, 0)
    ve, vw = beside(col_a, col_b, even_y, 1)
    turn[...] = jnp.zeros_like(turn)
    add_columns(
        u_in,
        u_out,
        (
            -c4 * nearest(*uw, -1) - q4 * slope(vw[0]),
            -c4 * next_one(uw[0], -1),
            -c4 * next_one(ue[0], 1),
            -c4 * nearest(*ue, 1) + q4 * slope(ve[0]),
        ),
        turn,
    )
    add_columns(
        v_in,
        v_out,
        (
            -c4 * nearest(*vw, -1) + q4 * (vw[1] - slope(uw[0])),
            -c4 * next_one(vw[0], -1) + q4 * vw[0],
            -c4 * next_one(ve[0], 1) + q4 * ve[0],
            -c4 * nearest(*ve, 1) + q4 * (ve[1] + slope(ue[0])),
        ),
        turn,
    )
    t_out[...] = t_in[...]
    lines = [corner_lines(obs, turn, f) for f in range(FIELDS)]
    none = jnp.zeros((LEV, CY), F32)
    for sign, this, other, near, far in ((-1, row_b, row_a, 1, 0), (1, row_a, row_b, 0, 1)):
        spot = 0 if sign < 0 else 2
        straight = [[outside(this, other, even_x, f, i) for f in range(2)] for i in (near, far)]
        corner = [[lines[f][spot + i] for f in range(FIELDS)] for i in (near, far)]
        both = [
            [tuple(p + q for p, q in zip(straight[i][f], corner[i][f])) for f in range(2)] for i in range(2)
        ]
        add_wind_rows(u_out, v_out, both[0], both[1], sign, coef[...], quarter[...])
        add_theta_rows(t_out, corner[0][2], corner[1][2], sign, coef[...], none)


def interpolate(start, obs, t, coef, table, model, block, row, col, lev, turn):
    far_up, near_up, near_down, far_down = corner_lines(obs, turn, 2)
    terms = (
        one(near_up, -1) + two(far_up, -1),
        two(near_up, -1),
        two(near_down, 1),
        one(near_down, 1) + two(far_down, 1),
    )
    lane = lax.broadcasted_iota(jnp.int32, (LEV, CY), 1)
    for r, term in zip(ROWS, terms):
        value = t[pl.ds(r, LEV, stride=CX), :] - coef[...] * term
        for c in (0, 1, CY - 2, CY - 1):
            to = (r >> 2) * 32 + (c >> 2)
            moved = pltpu.roll(value, (to - c) % CY, 1)
            high = moved.astype(BF16).astype(F32)
            at = ((r & 3) * 5 + (c & 3)) * LEV
            for k, part in enumerate((high, moved - high)):
                old = start[at : at + LEV, k * CY : (k + 1) * CY].astype(F32)
                table[at : at + LEV, k * CY : (k + 1) * CY] = jnp.where(lane == to, part, old).astype(BF16)
    owners = model.shape[0]
    cell = obs[:, 0, :].astype(jnp.int32)
    c, r = cell & (CY - 1), cell >> 7
    block[...] = (r >> 2) * 32 + (c >> 2)
    row[...] = r & 3
    col[...] = c & 3
    lev[...] = obs[:, 1, :].astype(jnp.int32)
    wide = 256
    block_iota = lax.broadcasted_iota(jnp.int32, (128, wide), 0)
    lev_iota = lax.broadcasted_iota(jnp.int32, (LEV, wide), 0)

    def pair(p, carry):
        def two(ref):
            return jnp.concatenate([ref[pl.ds(2 * p, 1), :], ref[pl.ds(2 * p + 1, 1), :]], axis=1)

        def sent(k):
            return jnp.concatenate([obs[2 * p, k : k + 1, :], obs[2 * p + 1, k : k + 1, :]], axis=1)

        def bit(value, mask):
            return jnp.broadcast_to(value & mask, (LEV, wide)) != 0

        at, r, c, l = two(block), two(row), two(col), two(lev)
        a, w0, w1 = sent(2), sent(3), sent(4)
        w2 = 1.0 - w0 - w1
        hot = jnp.where(block_iota == at, 1.0, 0.0).astype(BF16)
        got = jnp.dot(
            table[...], jnp.concatenate([hot, hot], axis=0), preferred_element_type=F32
        )
        c1, c2, r1, r2 = bit(c, 1), bit(c, 2), bit(r, 1), bit(r, 2)
        here, beside = [], []
        for i in range(5):
            g = [got[(i * 5 + j) * LEV : (i * 5 + j + 1) * LEV, :] for j in range(5 if i < 4 else 4)]
            h1 = jnp.where(c2, g[3], g[1])
            here.append(jnp.where(c1, h1, jnp.where(c2, g[2], g[0])))
            if i < 4:
                beside.append(jnp.where(c1, jnp.where(c2, g[4], g[2]), h1))
        h0, h1, h2 = (jnp.where(r2, here[i + 2], here[i]) for i in range(3))
        t0, t1 = jnp.where(r1, h1, h0), jnp.where(r1, h2, h1)
        t2 = jnp.where(
            r1, jnp.where(r2, beside[3], beside[1]), jnp.where(r2, beside[2], beside[0])
        )
        weight = jnp.where(lev_iota == l, 1.0 - a, jnp.where(lev_iota == l + 1, a, 0.0))
        out = jnp.sum(weight * (w0 * t0 + w1 * t1 + w2 * t2), axis=0, keepdims=True)
        model[pl.ds(2 * p, 1), :] = out[:, :128]
        model[pl.ds(2 * p + 1, 1), :] = out[:, 128:]
        return carry

    lax.fori_loop(0, owners // 2, pair, 0, unroll=UNROLL)


def swap(axis, first):
    count = lax.axis_size(axis)
    pairs = [((i + first) % count, (i + first + 1) % count) for i in range(0, count, 2)]
    return pairs + [(b, a) for a, b in pairs]


def on_device(theta, wind_u, wind_v, hyper, damp, cells, levels, bary, vfrac, values, mask):
    u, v, t = (f.reshape(FLAT, CY) for f in (wind_u, wind_v, theta))
    owners, slots = cells.shape[1], cells.shape[2]
    shape = jax.ShapeDtypeStruct
    sent = pl.pallas_call(
        messages_out,
        out_shape=shape((owners, SENT, slots), F32),
        in_specs=[HBM] * 7,
        out_specs=HBM,
        scratch_shapes=[
            pltpu.VMEM((FIELDS, FLAT, CY), F32),
            pltpu.VMEM((2, owners, slots), jnp.int32),
            pltpu.VMEM((owners, SENT, slots), F32),
            pltpu.VMEM((CY, CY), F32),
            pltpu.SemaphoreType.DMA((8,)),
        ],
        compiler_params=WHOLE,
        cost_estimate=cost(100000, 3000000),
    )(u, v, t, cells[0], levels[0], jnp.swapaxes(bary[0], 0, 1), vfrac[0])
    got = lax.all_to_all(sent, BOTH, split_axis=0, concat_axis=0, tiled=True)
    columns = shape((2 * BLOCKS, CY), F32)
    edge = shape((EDGE, CY), F32)
    own_a, own_b, row_a, row_b = pl.pallas_call(
        edges_out,
        out_shape=(columns, columns, edge, edge),
        in_specs=[VMEM] * 3,
        compiler_params=PARAMS,
        cost_estimate=cost(100000, 1000000),
    )(u, v, t)
    col_b = lax.ppermute(own_b, "py", swap("py", 1))
    col_a = lax.ppermute(own_a, "py", swap("py", 0))
    row_b = lax.ppermute(row_b, "px", swap("px", 1))
    row_a = lax.ppermute(row_a, "px", swap("px", 0))
    patch = shape((FLAT, CY), F32)
    plane = shape((LEV, CY), F32)
    grid = shape((24 * LEV, 2 * CY), BF16)
    turn = pltpu.VMEM((CY, CY), F32)
    u_part, v_part, t_part, pick, coef, quarter, across = pl.pallas_call(
        bulk,
        out_shape=(patch, patch, patch, shape((4 * CY, 4 * CY), BF16), plane, plane, shape((8, CY), F32)),
        in_specs=[VMEM] * 3 + [SMEM] * 2,
        compiler_params=PARAMS,
        cost_estimate=cost(8000000, 10000000),
    )(u, v, t, hyper, damp)
    t_most, table = pl.pallas_call(
        theta_borders,
        out_shape=(patch, grid),
        in_specs=[VMEM] * 11,
        scratch_shapes=[turn],
        compiler_params=PARAMS,
        cost_estimate=cost(4000000, 3000000),
    )(u, t_part, own_a, own_b, col_b, col_a, row_a, row_b, pick, coef, across)
    _, model = pl.pallas_call(
        interpolate,
        out_shape=(grid, shape((owners, slots), F32)),
        in_specs=[VMEM] * 4,
        scratch_shapes=[pltpu.VMEM((owners, slots), jnp.int32)] * 4 + [turn],
        input_output_aliases={0: 0},
        compiler_params=PARAMS,
        cost_estimate=cost(6500000000, 1000000),
    )(table, got, t_most, coef)
    u_next, v_next, t_next = pl.pallas_call(
        rest,
        out_shape=(patch, patch, patch),
        in_specs=[VMEM] * 11,
        scratch_shapes=[turn],
        compiler_params=PARAMS,
        cost_estimate=cost(4000000, 3000000),
    )(u_part, v_part, t_most, col_b, col_a, row_a, row_b, got, coef, quarter, across)
    back = lax.all_to_all(model, BOTH, split_axis=0, concat_axis=0, tiled=True)
    departures = mask.astype(F32) * (values - back[None])
    whole = theta.shape
    return t_next.reshape(whole), u_next.reshape(whole), v_next.reshape(whole), departures


def solution(mesh):
    field = P(None, "px", "py")
    obs = P(BOTH, None, None)
    return jax.shard_map(
        on_device,
        mesh=mesh,
        in_specs=(field, field, field, P(), P(), obs, obs, P(BOTH, None, None, None), obs, obs, obs),
        out_specs=(field, field, field, obs),
        check_vma=False,
    )
```
